512 devices in a mesh: slab: 16 (over y, x_lo, core), rep: 32 (over z, x_hi).
Axes of the slice: x: 4 (x_hi: 2, x_lo: 2; x = x_hi * 2 + x_lo), y: 4, z: 16, core: 2. Of those that a mesh axis runs over, the one named last changes fastest.
Arguments:
- cells: int32 [16, 65536], P('slab', 'rep'), may hold values from 0 to 262143
- charges: bfloat16 [16, 65536], P('slab', 'rep'), may hold values from 0.5 to 2
- counts: int32 [16, 32], P('slab', 'rep'), may hold values from 1 to 2048, 49152 in all within a row
- potential_guess: float32 [256, 128, 128], P('slab'), may hold values from -6 to 6
Outputs:
- kicks: float32 [3, 16, 65536], P(None, 'slab', 'rep')
The draws below stay inside these ranges and needn't reach their ends.
Inputs may be any that keep to these rules, and one draw needn't show every extreme that they name: `cells`: a cell is (iz * 128 + ix) * 128 + iy within the macroparticle's own slab. The first counts[s, r] of the 2048 slots of device (s, r) are live; some device holds exactly 2048.
All inputs are finite; a program needn't handle non-finite values.
Results may differ from the reference program's by a relative error of at most 0.003.
Values may be sent and summed in bfloat16 or wider, within the bound.
A program may use at most 64 MiB of HBM per device.

```python
import math
import jax
import jax.numpy as jnp
import numpy as np

NXG = 128
NYG = 128
PART_DEV = 2048
SWEEPS = 8
SLABS = 16
REPLICAS = 32
NZ = 256
CELLS = 262144


def plant(drawn, own_key, smallest, high):
    dims = drawn.shape
    index_at = [jax.random.randint(jax.random.fold_in(own_key, axis), (), 0, dims[axis]) for axis in range(len(dims))]
    drawn = drawn.at[tuple(index_at)].set(smallest)
    longest = dims.index(max(dims))
    index_at[longest] = (index_at[longest] + 1) % dims[longest]
    return drawn.at[tuple(index_at)].set(high)


def level_of(stream_key, extent, pieces, least, largest):
    def one(dim, shards_of):
        heights = jax.random.uniform(jax.random.fold_in(jax.random.fold_in(stream_key, 6), dim), (shards_of,), jnp.float32, least / len(pieces), largest / len(pieces))
        return jnp.repeat(jnp.exp(heights), extent[dim] // shards_of).reshape((-1,) + (1,) * (len(extent) - dim - 1))

    gain = one(*pieces[0])
    for cut in pieces[1:]:
        gain = gain * one(*cut)
    return gain


def split_up(count, total, limit, skew):
    loads = [(1 << 20) // math.isqrt(standing ** skew) + 1 for standing in range(2, count + 1)]
    rest, given = total - limit - (count - 1), [1] * (count - 1)
    while rest > 0:
        candidates = [i for i in range(count - 1) if given[i] < limit]
        whole, budget = sum([loads[i] for i in candidates]), rest
        for i in candidates:
            more = min(limit - given[i], max(1, budget * loads[i] // whole), rest)
            given[i] = given[i] + more
            rest = rest - more
    return np.array([limit] + given)


def ragged_sizes(rng, amount, total, reach, slope):
    if amount == 2:
        one = jax.random.randint(rng, (), max(1, total - reach), min(reach, total - 1) + 1)
        return jnp.stack([one, total - one])
    sizes = jnp.asarray(split_up(amount, total, reach, slope), jnp.int32)
    pairs = (amount - 1) // 2
    source_of, taker = sizes[1:1 + 2 * pairs:2], sizes[2:2 + 2 * pairs:2]
    slack = jnp.minimum(source_of - 1, reach - taker)
    passed = jax.random.randint(jax.random.fold_in(rng, 1), (pairs,), 0, 1 << 20) % (slack + 1)
    sizes = sizes.at[1:1 + 2 * pairs:2].set(source_of - passed).at[2:2 + 2 * pairs:2].set(taker + passed)
    return sizes[jax.random.permutation(jax.random.fold_in(rng, 2), amount)]


def noise(own_key, shape, spread, most, split=(), kind=jnp.bfloat16):
    drawn = jax.random.normal(own_key, shape, jnp.float32) * spread
    if len(split) > 0:
        drawn = level_of(own_key, shape, split, -0.22, 0.18) * drawn
    return jnp.clip(drawn, min=-most, max=most).astype(kind)


def setup_inputs(seed: int = 0) -> dict:
    key_list = jax.random.split(jax.random.key(seed), 5)
    cells = plant(jax.random.randint(key_list[0], (SLABS, REPLICAS * PART_DEV), 0, CELLS), jax.random.fold_in(key_list[0], 1), 0, CELLS - 1).astype(jnp.int32)
    charges = jnp.clip(jnp.exp(math.log(2.0) - 1.3862944 * jax.random.uniform(key_list[1], (SLABS, REPLICAS * PART_DEV), jnp.float32) ** level_of(key_list[1], (SLABS, REPLICAS * PART_DEV), ((0, 16), (1, 32)), -0.2, 0.2)), 0.5, 2.0).astype(jnp.bfloat16)
    counts = jax.vmap(lambda own: ragged_sizes(own, REPLICAS, REPLICAS * PART_DEV * 3 // 4, PART_DEV, 1))(jax.random.split(key_list[2], SLABS)).reshape((SLABS, REPLICAS)).astype(jnp.int32)
    potential_guess = noise(key_list[3], (NZ, NXG, NYG), 1.0, 6.0, ((0, 16),), jnp.float32)
    return dict(cells=cells, charges=charges, counts=counts, potential_guess=potential_guess)


SCREEN_TERM = 0.05
KICK_STRENGTH = 1.0


def operate(field):
    diag = 6.0 + SCREEN_TERM
    cycle_sum = jnp.roll(field, 1, axis=0) + jnp.roll(field, -1, axis=0)
    padded = jnp.pad(field, ((0, 0), (1, 1), (1, 1)))
    beside = padded[:, 2:, 1:-1] + padded[:, :-2, 1:-1] + padded[:, 1:-1, 2:] + padded[:, 1:-1, :-2]
    return diag * field - (cycle_sum + beside)


def chebyshev(charge_grid, guess):
    diag = 6.0 + SCREEN_TERM
    lower = SCREEN_TERM / diag
    upper = (12.0 + SCREEN_TERM) / diag
    centre = (upper + lower) / 2.0
    radius = (upper - lower) / 2.0
    sigma_ratio = centre / radius
    rho_coef = 1.0 / sigma_ratio
    residual = charge_grid - operate(guess)
    step_field = residual / (diag * centre)
    potential = guess
    for sweep_index in range(SWEEPS):
        potential = potential + step_field
        if sweep_index < SWEEPS - 1:
            residual = residual - operate(step_field)
            rho_next = 1.0 / (2.0 * sigma_ratio - rho_coef)
            step_field = rho_next * rho_coef * step_field + (2.0 * rho_next / radius) * (residual / diag)
            rho_coef = rho_next
    return potential


def reference(cells, charges, counts, potential_guess):
    slots = jnp.arange(PART_DEV, dtype=jnp.int32)
    live_mask = (slots[None, None, :] < counts[:, :, None]).reshape(SLABS, REPLICAS * PART_DEV)
    slab_base = (jnp.arange(SLABS, dtype=jnp.int32) * CELLS)[:, None]
    global_index = (cells + slab_base).reshape(-1)
    weights = jnp.where(live_mask, charges.astype(jnp.float32), jnp.float32(0.0)).reshape(-1)
    charge_grid = jax.ops.segment_sum(weights, global_index, num_segments=NZ * NXG * NYG)
    charge_grid = charge_grid.reshape(NZ, NXG, NYG)
    potential = chebyshev(charge_grid, potential_guess)
    padded = jnp.pad(potential, ((0, 0), (1, 1), (1, 1)))
    field_x = -(padded[:, 2:, 1:-1] - padded[:, :-2, 1:-1]) * 0.5
    field_y = -(padded[:, 1:-1, 2:] - padded[:, 1:-1, :-2]) * 0.5
    field_z = -(jnp.roll(potential, -1, axis=0) - jnp.roll(potential, 1, axis=0)) * 0.5
    fields = jnp.stack([field_x, field_y, field_z], axis=0).astype(jnp.bfloat16)
    flat_fields = fields.reshape(3, NZ * NXG * NYG)
    values = jnp.take(flat_fields, global_index, axis=1).astype(jnp.float32)
    values = values.reshape(3, SLABS, REPLICAS * PART_DEV)
    return KICK_STRENGTH * jnp.where(live_mask[None], values, jnp.float32(0.0))
```

```python
import jax
import jax.numpy as jnp
from jax import lax
from jax.experimental import pallas as pl
from jax.experimental.pallas import tpu as pltpu
from jax.sharding import PartitionSpec as P

SWEEPS = 8
SCREEN_TERM = 0.05
KICK_STRENGTH = 1.0
DIAG = 6.0 + SCREEN_TERM
PAD = 8
LANES = 128
VMEM_LIMIT = 60 * 1024 * 1024


def coefficients():
    lower = SCREEN_TERM / DIAG
    upper = (12.0 + SCREEN_TERM) / DIAG
    centre = (upper + lower) / 2.0
    radius = (upper - lower) / 2.0
    sigma_ratio = centre / radius
    rho = 1.0 / sigma_ratio
    push = 1.0 / (DIAG * centre)
    result = [(1.0 - push * DIAG, 0.0, push)]
    for _ in range(SWEEPS - 1):
        rho_next = 1.0 / (2.0 * sigma_ratio - rho)
        alpha = rho_next * rho
        push = 2.0 * rho_next / radius / DIAG
        result.append((1.0 + alpha - push * DIAG, alpha, push))
        rho = rho_next
    return result


def deposit_kernel(counts_ref, cells_ref, charges_ref, out_ref):
    total = cells_ref.shape[1]
    rows = out_ref.shape[0]
    cells = cells_ref[...]
    live = lax.broadcasted_iota(jnp.int32, (1, total), 1) < counts_ref[0, 0]
    weights = jnp.where(live, charges_ref[...].astype(jnp.float32), 0.0)
    column = cells & (LANES - 1)
    row = cells >> 7
    spread = jnp.where(
        lax.broadcasted_iota(jnp.int32, (LANES, total), 0) == column, weights, 0.0
    ).astype(jnp.bfloat16)
    block = 256
    iota = lax.broadcasted_iota(jnp.int32, (block, total), 0)
    for start in range(0, rows, block):
        onehot = jnp.where(iota == row - start, 1.0, 0.0).astype(jnp.bfloat16)
        out_ref[start : start + block, :] = lax.dot_general(
            onehot, spread, (((1,), (1,)), ((), ())), preferred_element_type=jnp.float32
        ).astype(out_ref.dtype)


def solve_kernel(
    counts_ref,
    cells_ref,
    guess_ref,
    guess_before_ref,
    guess_after_ref,
    charge_ref,
    charge_before_ref,
    charge_after_ref,
    out_ref,
    even,
    odd,
    charge,
    table,
):
    planes, side, _ = guess_ref.shape
    depth = guess_before_ref.shape[0]
    total = cells_ref.shape[1]
    inside = pl.ds(PAD, side)

    blank = jnp.zeros((PAD, LANES), jnp.float32)

    @pl.loop(0, planes + 2 * depth)
    def _(plane):
        for buffer in (even, odd):
            buffer[plane, pl.ds(0, PAD), :] = blank
            buffer[plane, pl.ds(PAD + side, PAD), :] = blank

    @pl.loop(0, depth)
    def _(plane):
        even[plane, inside, :] = guess_before_ref[plane]
        even[depth + planes + plane, inside, :] = guess_after_ref[plane]

    @pl.loop(0, planes)
    def _(plane):
        even[depth + plane, inside, :] = guess_ref[plane]
        charge[depth - 1 + plane] = charge_ref[plane].astype(jnp.float32)

    @pl.loop(0, depth - 1)
    def _(plane):
        charge[plane] = charge_before_ref[plane].astype(jnp.float32)
        charge[depth - 1 + planes + plane] = charge_after_ref[plane].astype(jnp.float32)

    lane = lax.broadcasted_iota(jnp.int32, (side, LANES), 1)
    first, last = lane == 0, lane == LANES - 1

    def beside(value):
        left = jnp.where(first, 0.0, pltpu.roll(value, 1, 1))
        right = jnp.where(last, 0.0, pltpu.roll(value, LANES - 1, 1))
        return left, right

    buffers = (even, odd)
    for sweep, (keep, previous, push) in enumerate(coefficients()):
        now, later = buffers[sweep % 2], buffers[(sweep + 1) % 2]

        @pl.loop(sweep + 1, planes + 2 * depth - 1 - sweep, unroll=2)
        def _(plane):
            value = now[plane, inside, :]
            left, right = beside(value)
            around = (left + right) + (
                now[plane, pl.ds(PAD - 1, side), :] + now[plane, pl.ds(PAD + 1, side), :]
            )
            around = around + (now[plane - 1, inside, :] + now[plane + 1, inside, :])
            fresh = keep * value + push * (charge[plane - 1] + around)
            if sweep:
                fresh = fresh - previous * later[plane, inside, :]
            later[plane, inside, :] = fresh

    final = buffers[SWEEPS % 2]
    for plane in range(planes):
        at = depth + plane
        spot = slice(plane * LANES, (plane + 1) * LANES)
        left, right = beside(final[at, inside, :])
        parts = (
            final[at, pl.ds(PAD - 1, side), :] - final[at, pl.ds(PAD + 1, side), :],
            left - right,
            final[at - 1, inside, :] - final[at + 1, inside, :],
        )
        for part, difference in enumerate(parts):
            table[part * side : (part + 1) * side, spot] = (difference * 0.5).astype(jnp.bfloat16)

    block = 256
    keys = lax.broadcasted_iota(jnp.int32, (planes * LANES, block), 0)
    ranks = lax.broadcasted_iota(jnp.int32, (side, block), 0)
    for start in range(0, total, block):
        cells = cells_ref[:, start : start + block]
        key = ((cells >> 14) << 7) | (cells & (LANES - 1))
        rank = (cells >> 7) & (LANES - 1)
        onehot = jnp.where(keys == key, 1.0, 0.0).astype(jnp.bfloat16)
        picked = jnp.dot(table[...], onehot, preferred_element_type=jnp.float32)
        slot = lax.broadcasted_iota(jnp.int32, (1, block), 1) + start
        live = slot < counts_ref[0, 0]
        chosen = (ranks == rank) & live
        for part in range(3):
            values = jnp.where(chosen, picked[part * side : (part + 1) * side], 0.0)
            out_ref[part : part + 1, start : start + block] = KICK_STRENGTH * jnp.sum(
                values, axis=0, keepdims=True
            )


def local(cells, charges, counts, potential_guess):
    planes, side, _ = potential_guess.shape
    total = cells.shape[1]
    count = lax.axis_size("slab")
    up = [(i, (i + 1) % count) for i in range(count)]
    down = [(j, i) for i, j in up]
    depth = SWEEPS + 1
    vmem = pl.BlockSpec(memory_space=pltpu.VMEM)
    smem = pl.BlockSpec(memory_space=pltpu.SMEM)
    params = pltpu.CompilerParams(vmem_limit_bytes=VMEM_LIMIT)

    guess_before = lax.ppermute(potential_guess[planes - depth :], "slab", up)
    guess_after = lax.ppermute(potential_guess[:depth], "slab", down)
    deposited = pl.pallas_call(
        deposit_kernel,
        out_shape=jax.ShapeDtypeStruct((planes * side, LANES), jnp.bfloat16),
        in_specs=[smem, vmem, vmem],
        out_specs=vmem,
        compiler_params=params,
        cost_estimate=pl.CostEstimate(flops=2 * planes * side * LANES * total, bytes_accessed=2**19, transcendentals=0),
    )(counts, cells, charges)
    charge = lax.psum(deposited, "rep").reshape(planes, side, LANES)
    charge_before = lax.ppermute(charge[planes - depth + 1 :], "slab", up)
    charge_after = lax.ppermute(charge[: depth - 1], "slab", down)
    deep = planes + 2 * depth
    kicks = pl.pallas_call(
        solve_kernel,
        out_shape=jax.ShapeDtypeStruct((3, total), jnp.float32),
        in_specs=[smem] + [vmem] * 7,
        out_specs=vmem,
        scratch_shapes=[
            pltpu.VMEM((deep, side + 2 * PAD, LANES), jnp.float32),
            pltpu.VMEM((deep, side + 2 * PAD, LANES), jnp.float32),
            pltpu.VMEM((deep - 2, side, LANES), jnp.float32),
            pltpu.VMEM((3 * side, planes * LANES), jnp.bfloat16),
        ],
        compiler_params=params,
    )(counts, cells, potential_guess, guess_before, guess_after, charge, charge_before, charge_after)
    return kicks.reshape(3, 1, total)


def solution(mesh):
    return jax.shard_map(
        local,
        mesh=mesh,
        in_specs=(P("slab", "rep"), P("slab", "rep"), P("slab", "rep"), P("slab", None, None)),
        out_specs=P(None, "slab", "rep"),
        check_vma=False,
    )
```

```python
import jax
import jax.numpy as jnp
from jax import lax
from jax.experimental import pallas as pl
from jax.experimental.pallas import tpu as pltpu
from jax.sharding import PartitionSpec as P

SWEEPS = 8
SCREEN_TERM = 0.05
KICK_STRENGTH = 1.0
DIAG = 6.0 + SCREEN_TERM
PAD = 8
LANES = 128
VMEM_LIMIT = 60 * 1024 * 1024


def coefficients():
    lower = SCREEN_TERM / DIAG
    upper = (12.0 + SCREEN_TERM) / DIAG
    centre = (upper + lower) / 2.0
    radius = (upper - lower) / 2.0
    sigma_ratio = centre / radius
    rho = 1.0 / sigma_ratio
    push = 1.0 / (DIAG * centre)
    result = [(1.0 - push * DIAG, 0.0, push)]
    for _ in range(SWEEPS - 1):
        rho_next = 1.0 / (2.0 * sigma_ratio - rho)
        alpha = rho_next * rho
        push = 2.0 * rho_next / radius / DIAG
        result.append((1.0 + alpha - push * DIAG, alpha, push))
        rho = rho_next
    return result


def deposit_kernel(counts_ref, cells_ref, charges_ref, out_ref):
    total = cells_ref.shape[1]
    rows = out_ref.shape[0]
    cells = cells_ref[...]
    live = lax.broadcasted_iota(jnp.int32, (1, total), 1) < counts_ref[0, 0]
    weights = jnp.where(live, charges_ref[...].astype(jnp.float32), 0.0)
    column = cells & (LANES - 1)
    row = cells >> 7
    spread = jnp.where(
        lax.broadcasted_iota(jnp.int32, (LANES, total), 0) == column, weights, 0.0
    ).astype(jnp.bfloat16)
    block = 256
    iota = lax.broadcasted_iota(jnp.int32, (block, total), 0)
    for start in range(0, rows, block):
        onehot = jnp.where(iota == row - start, 1.0, 0.0).astype(jnp.bfloat16)
        out_ref[start : start + block, :] = lax.dot_general(
            onehot, spread, (((1,), (1,)), ((), ())), preferred_element_type=jnp.float32
        ).astype(out_ref.dtype)


CLASS_ROWS = 256
HALF = CLASS_ROWS // 2
NEAR = (
    (2, 0, 0, HALF, 5),
    (2, 1, 0, HALF, 6),
    (-2, 0, HALF, HALF, 5),
    (-2, 1, HALF, HALF, 6),
    (0, 1, 0, CLASS_ROWS, 0),
    (1, 1, 0, CLASS_ROWS, 2),
    (-1, 1, 0, CLASS_ROWS, 4),
    (1, 0, 0, CLASS_ROWS, 1),
    (-1, 0, 0, CLASS_ROWS, 3),
)
NEAR_SLOTS = 7
FAR = (2, 1, 3)
MESH = pl.DeviceIdType.MESH


def reduce_kernel(
    partial_ref,
    guess_ref,
    charge_ref,
    charge_before_ref,
    charge_after_ref,
    guess_before_ref,
    guess_after_ref,
    near_in,
    far_in,
    near_sum,
    near_send,
    near_recv,
    far_send,
    far_recv,
    spread_send,
    spread_recv,
    last_send,
    last_recv,
    halo_send,
    halo_recv,
):
    ring = lax.axis_size("rep") // 2
    rep = lax.axis_index("rep")
    z, x = rep // 2, lax.rem(rep, 2)
    slabs = lax.axis_size("slab")
    slab = lax.axis_index("slab")
    above, below = lax.rem(slab + 1, slabs), lax.rem(slab + slabs - 1, slabs)
    planes = guess_ref.shape[0]
    depth = guess_before_ref.shape[0]
    half = charge_after_ref.shape[0]
    piece = CLASS_ROWS // 4

    def place(step, other):
        return lax.rem(z + step + ring, ring), (1 - x if other else x)

    def rep_of(step, other):
        to_z, to_x = place(step, other)
        return to_z * 2 + to_x

    def class_of(step, other):
        to_z, to_x = place(step, other)
        return pl.multiple_of((lax.rem(to_z, 4) * 2 + to_x) * CLASS_ROWS, CLASS_ROWS)

    def send(src, dst, send_sem, recv_sem, **target):
        copy = pltpu.make_async_remote_copy(
            src_ref=src, dst_ref=dst, send_sem=send_sem, recv_sem=recv_sem,
            device_id=target, device_id_type=MESH,
        )
        copy.start()
        return copy

    barrier = pltpu.get_barrier_semaphore()
    for step in FAR:
        pl.semaphore_signal(barrier, inc=1, device_id={"rep": rep_of(4 * step, 0)}, device_id_type=MESH)
    for step, other, _, _, _ in NEAR:
        pl.semaphore_signal(barrier, inc=1, device_id={"rep": rep_of(step, other)}, device_id_type=MESH)
    for target in (above, below):
        pl.semaphore_signal(barrier, inc=1, device_id={"slab": target}, device_id_type=MESH)
    pl.semaphore_wait(barrier, len(FAR) + len(NEAR) + 2)

    near = [
        send(
            partial_ref.at[pl.ds(class_of(step, other) + first, rows)],
            near_in.at[slot, pl.ds(first, rows)],
            near_send.at[i], near_recv.at[i], rep=rep_of(step, other),
        )
        for i, (step, other, first, rows, slot) in enumerate(NEAR)
    ]
    halo = [
        send(guess_ref.at[pl.ds(planes - depth, depth)], guess_before_ref, halo_send.at[0], halo_recv.at[0], slab=above),
        send(guess_ref.at[pl.ds(0, depth)], guess_after_ref, halo_send.at[1], halo_recv.at[1], slab=below),
    ]
    for copy in near:
        copy.wait_recv()
    mine = class_of(0, 0)
    total = partial_ref[pl.ds(mine, CLASS_ROWS), :].astype(jnp.float32)
    for slot in range(NEAR_SLOTS):
        total = total + near_in[slot].astype(jnp.float32)
    near_sum[...] = total.astype(near_sum.dtype)

    lot = z // 4
    far = []
    for i, step in enumerate(FAR):
        start = pl.multiple_of(lax.rem(lot + step, 4) * piece, piece)
        far.append(
            send(near_sum.at[pl.ds(start, piece)], far_in.at[i], far_send.at[i], far_recv.at[i], rep=rep_of(4 * step, 0))
        )
    for copy in far:
        copy.wait_recv()
    own = pl.multiple_of(lot * piece, piece)
    total = near_sum[pl.ds(own, piece), :].astype(jnp.float32)
    for i in range(len(FAR)):
        total = total + far_in[i].astype(jnp.float32)
    spot = pl.ds(pl.multiple_of(mine + own, piece), piece)
    charge_ref[spot, :] = total.astype(charge_ref.dtype)

    spreads = [
        send(charge_ref.at[spot], charge_ref.at[spot], spread_send.at[i], spread_recv.at[i], rep=rep_of(4 * step, 0))
        for i, step in enumerate(FAR)
    ]
    for copy in spreads:
        copy.wait_recv()
    lasts = []
    for i, (step, other, first, rows, _) in enumerate(NEAR):
        block = charge_ref.at[pl.ds(mine + first, rows)]
        lasts.append(send(block, block, last_send.at[i], last_recv.at[i], rep=rep_of(step, other)))
    for copy in lasts:
        copy.wait_recv()
    halo.append(
        send(charge_ref.at[pl.ds(half, half)], charge_before_ref, halo_send.at[2], halo_recv.at[2], slab=above)
    )
    halo.append(
        send(charge_ref.at[pl.ds(0, half)], charge_after_ref, halo_send.at[3], halo_recv.at[3], slab=below)
    )
    for copy in halo:
        copy.wait_recv()
    for copy in near + far + spreads + lasts + halo:
        copy.wait_send()


def solve_kernel(
    counts_ref,
    cells_ref,
    guess_ref,
    guess_before_ref,
    guess_after_ref,
    charge_ref,
    charge_before_ref,
    charge_after_ref,
    out_ref,
    even,
    odd,
    charge,
    table,
):
    planes, side, _ = guess_ref.shape
    depth = guess_before_ref.shape[0]
    total = cells_ref.shape[1]
    inside = pl.ds(PAD, side)

    blank = jnp.zeros((PAD, LANES), jnp.float32)

    @pl.loop(0, planes + 2 * depth)
    def _(plane):
        for buffer in (even, odd):
            buffer[plane, pl.ds(0, PAD), :] = blank
            buffer[plane, pl.ds(PAD + side, PAD), :] = blank

    @pl.loop(0, depth)
    def _(plane):
        even[plane, inside, :] = guess_before_ref[plane]
        even[depth + planes + plane, inside, :] = guess_after_ref[plane]

    @pl.loop(0, planes)
    def _(plane):
        even[depth + plane, inside, :] = guess_ref[plane]
        charge[depth - 1 + plane] = charge_ref[plane].astype(jnp.float32)

    @pl.loop(0, depth - 1)
    def _(plane):
        charge[plane] = charge_before_ref[plane].astype(jnp.float32)
        charge[depth - 1 + planes + plane] = charge_after_ref[plane].astype(jnp.float32)

    lane = lax.broadcasted_iota(jnp.int32, (side, LANES), 1)
    first, last = lane == 0, lane == LANES - 1

    def beside(value):
        left = jnp.where(first, 0.0, pltpu.roll(value, 1, 1))
        right = jnp.where(last, 0.0, pltpu.roll(value, LANES - 1, 1))
        return left, right

    buffers = (even, odd)
    for sweep, (keep, previous, push) in enumerate(coefficients()):
        now, later = buffers[sweep % 2], buffers[(sweep + 1) % 2]

        @pl.loop(sweep + 1, planes + 2 * depth - 1 - sweep, unroll=2)
        def _(plane):
            value = now[plane, inside, :]
            left, right = beside(value)
            around = (left + right) + (
                now[plane, pl.ds(PAD - 1, side), :] + now[plane, pl.ds(PAD + 1, side), :]
            )
            around = around + (now[plane - 1, inside, :] + now[plane + 1, inside, :])
            fresh = keep * value + push * (charge[plane - 1] + around)
            if sweep:
                fresh = fresh - previous * later[plane, inside, :]
            later[plane, inside, :] = fresh

    final = buffers[SWEEPS % 2]
    for plane in range(planes):
        at = depth + plane
        spot = slice(plane * LANES, (plane + 1) * LANES)
        left, right = beside(final[at, inside, :])
        parts = (
            final[at, pl.ds(PAD - 1, side), :] - final[at, pl.ds(PAD + 1, side), :],
            left - right,
            final[at - 1, inside, :] - final[at + 1, inside, :],
        )
        for part, difference in enumerate(parts):
            table[part * side : (part + 1) * side, spot] = (difference * 0.5).astype(jnp.bfloat16)

    block = 256
    keys = lax.broadcasted_iota(jnp.int32, (planes * LANES, block), 0)
    ranks = lax.broadcasted_iota(jnp.int32, (side, block), 0)
    for start in range(0, total, block):
        cells = cells_ref[:, start : start + block]
        key = ((cells >> 14) << 7) | (cells & (LANES - 1))
        rank = (cells >> 7) & (LANES - 1)
        onehot = jnp.where(keys == key, 1.0, 0.0).astype(jnp.bfloat16)
        picked = jnp.dot(table[...], onehot, preferred_element_type=jnp.float32)
        slot = lax.broadcasted_iota(jnp.int32, (1, block), 1) + start
        live = slot < counts_ref[0, 0]
        chosen = (ranks == rank) & live
        for part in range(3):
            values = jnp.where(chosen, picked[part * side : (part + 1) * side], 0.0)
            out_ref[part, :, start : start + block] = KICK_STRENGTH * jnp.sum(
                values, axis=0, keepdims=True
            )


def local(cells, charges, counts, potential_guess):
    planes, side, _ = potential_guess.shape
    total = cells.shape[1]
    depth = SWEEPS + 1
    vmem = pl.BlockSpec(memory_space=pltpu.VMEM)
    smem = pl.BlockSpec(memory_space=pltpu.SMEM)
    params = pltpu.CompilerParams(vmem_limit_bytes=VMEM_LIMIT)

    deposited = pl.pallas_call(
        deposit_kernel,
        out_shape=jax.ShapeDtypeStruct((planes * side, LANES), jnp.bfloat16),
        in_specs=[smem, vmem, vmem],
        out_specs=vmem,
        compiler_params=params,
        cost_estimate=pl.CostEstimate(flops=2 * planes * side * LANES * total, bytes_accessed=2**19, transcendentals=0),
    )(counts, cells, charges)
    rows = planes * side
    half = (depth - 1) * side
    near = pltpu.SemaphoreType.DMA((len(NEAR),))
    far = pltpu.SemaphoreType.DMA((len(FAR),))
    ends = pltpu.SemaphoreType.DMA((4,))
    charge, charge_before, charge_after, guess_before, guess_after = pl.pallas_call(
        reduce_kernel,
        out_shape=[
            jax.ShapeDtypeStruct((rows, LANES), jnp.bfloat16),
            jax.ShapeDtypeStruct((half, LANES), jnp.bfloat16),
            jax.ShapeDtypeStruct((half, LANES), jnp.bfloat16),
            jax.ShapeDtypeStruct((depth, side, LANES), jnp.float32),
            jax.ShapeDtypeStruct((depth, side, LANES), jnp.float32),
        ],
        in_specs=[vmem] * 2,
        out_specs=[vmem] * 5,
        scratch_shapes=[
            pltpu.VMEM((NEAR_SLOTS, CLASS_ROWS, LANES), jnp.bfloat16),
            pltpu.VMEM((len(FAR), CLASS_ROWS // 4, LANES), jnp.bfloat16),
            pltpu.VMEM((CLASS_ROWS, LANES), jnp.bfloat16),
            near, near, far, far, far, far, near, near, ends, ends,
        ],
        compiler_params=pltpu.CompilerParams(
            vmem_limit_bytes=VMEM_LIMIT, collective_id=0, has_side_effects=True
        ),
    )(deposited, potential_guess)
    charge = charge.reshape(planes, side, LANES)
    charge_before = charge_before.reshape(depth - 1, side, LANES)
    charge_after = charge_after.reshape(depth - 1, side, LANES)
    deep = planes + 2 * depth
    kicks = pl.pallas_call(
        solve_kernel,
        out_shape=jax.ShapeDtypeStruct((3, 1, total), jnp.float32),
        in_specs=[smem] + [vmem] * 7,
        out_specs=vmem,
        scratch_shapes=[
            pltpu.VMEM((deep, side + 2 * PAD, LANES), jnp.float32),
            pltpu.VMEM((deep, side + 2 * PAD, LANES), jnp.float32),
            pltpu.VMEM((deep - 2, side, LANES), jnp.float32),
            pltpu.VMEM((3 * side, planes * LANES), jnp.bfloat16),
        ],
        compiler_params=params,
    )(counts, cells, potential_guess, guess_before, guess_after, charge, charge_before, charge_after)
    return kicks


def solution(mesh):
    return jax.shard_map(
        local,
        mesh=mesh,
        in_specs=(P("slab", "rep"), P("slab", "rep"), P("slab", "rep"), P("slab", None, None)),
        out_specs=P(None, "slab", "rep"),
        check_vma=False,
    )
```

```python
import jax
import jax.numpy as jnp
from jax import lax
from jax.experimental import pallas as pl
from jax.experimental.pallas import tpu as pltpu
from jax.sharding import PartitionSpec as P

SWEEPS = 8
SCREEN_TERM = 0.05
KICK_STRENGTH = 1.0
DIAG = 6.0 + SCREEN_TERM
PAD = 8
LANES = 128
VMEM_LIMIT = 60 * 1024 * 1024


def coefficients():
    lower = SCREEN_TERM / DIAG
    upper = (12.0 + SCREEN_TERM) / DIAG
    centre = (upper + lower) / 2.0
    radius = (upper - lower) / 2.0
    sigma_ratio = centre / radius
    rho = 1.0 / sigma_ratio
    push = 1.0 / (DIAG * centre)
    result = [(1.0 - push * DIAG, 0.0, push)]
    for _ in range(SWEEPS - 1):
        rho_next = 1.0 / (2.0 * sigma_ratio - rho)
        alpha = rho_next * rho
        push = 2.0 * rho_next / radius / DIAG
        result.append((1.0 + alpha - push * DIAG, alpha, push))
        rho = rho_next
    return result


def deposit(counts_ref, cells_ref, charges_ref, out_ref):
    total = cells_ref.shape[1]
    rows = out_ref.shape[0]
    cells = cells_ref[...]
    live = lax.broadcasted_iota(jnp.int32, (1, total), 1) < counts_ref[0, 0]
    weights = jnp.where(live, charges_ref[...].astype(jnp.float32), 0.0)
    column = cells & (LANES - 1)
    row = cells >> 7
    spread = jnp.where(
        lax.broadcasted_iota(jnp.int32, (LANES, total), 0) == column, weights, 0.0
    ).astype(jnp.bfloat16)
    block = 256
    iota = lax.broadcasted_iota(jnp.int32, (block, total), 0)
    for start in range(0, rows, block):
        onehot = jnp.where(iota == row - start, 1.0, 0.0).astype(jnp.bfloat16)
        out_ref[start : start + block, :] = lax.dot_general(
            onehot, spread, (((1,), (1,)), ((), ())), preferred_element_type=jnp.float32
        ).astype(out_ref.dtype)


CLASS_ROWS = 512
HALF = CLASS_ROWS // 2
NEAR = ((2, 0, HALF, 2), (-2, HALF, HALF, 2), (1, 0, CLASS_ROWS, 0), (-1, 0, CLASS_ROWS, 1))
NEAR_SLOTS = 3
FAR = ((2, 1), (2, 0), (1, 1), (3, 1), (1, 0), (3, 0), (0, 1))
PIECE = CLASS_ROWS // 8
MESH = pl.DeviceIdType.MESH


def reduce_kernel(
    counts_ref,
    cells_ref,
    charges_ref,
    guess_ref,
    charge_ref,
    halo_ref,
    guess_before_ref,
    guess_after_ref,
    partial_ref,
    near_in,
    near_sum,
    far_in,
    near_send,
    near_recv,
    far_send,
    far_recv,
    spread_send,
    spread_recv,
    last_send,
    last_recv,
    halo_send,
    halo_recv,
    guess_send,
    guess_recv,
):
    ring = lax.axis_size("rep") // 2
    rep = lax.axis_index("rep")
    z, x = rep // 2, lax.rem(rep, 2)
    slabs = lax.axis_size("slab")
    slab = lax.axis_index("slab")
    above, below = lax.rem(slab + 1, slabs), lax.rem(slab + slabs - 1, slabs)
    planes = guess_ref.shape[0]
    depth = guess_before_ref.shape[0]
    middle = charge_ref.shape[0] // 2

    def rep_of(step, other=0):
        return lax.rem(z + step + ring, ring) * 2 + (1 - x if other else x)

    def class_of(step):
        return pl.multiple_of(lax.rem(z + step + ring, 4) * CLASS_ROWS, CLASS_ROWS)

    def piece_of(step, other):
        lot = lax.rem(z // 4 + step, 4) * 2 + (1 - x if other else x)
        return pl.multiple_of(lot * PIECE, PIECE)

    def send(src, dst, send_sem, recv_sem, **target):
        copy = pltpu.make_async_remote_copy(
            src_ref=src, dst_ref=dst, send_sem=send_sem, recv_sem=recv_sem,
            device_id=target, device_id_type=MESH,
        )
        copy.start()
        return copy

    barrier = pltpu.get_barrier_semaphore()
    for step, other in FAR:
        pl.semaphore_signal(barrier, inc=1, device_id={"rep": rep_of(4 * step, other)}, device_id_type=MESH)
    for step, _, _, _ in NEAR:
        pl.semaphore_signal(barrier, inc=1, device_id={"rep": rep_of(step)}, device_id_type=MESH)
    for target in (above, below):
        pl.semaphore_signal(barrier, inc=1, device_id={"slab": target}, device_id_type=MESH)

    deposit(counts_ref, cells_ref, charges_ref, partial_ref)
    pl.semaphore_wait(barrier, len(FAR) + len(NEAR) + 2)

    near = [
        send(
            partial_ref.at[pl.ds(class_of(step) + first, rows)],
            near_in.at[slot, pl.ds(first, rows)],
            near_send.at[i], near_recv.at[i], rep=rep_of(step),
        )
        for i, (step, first, rows, slot) in enumerate(NEAR)
    ]
    guesses = [
        send(guess_ref.at[pl.ds(planes - depth, depth)], guess_before_ref, guess_send.at[0], guess_recv.at[0], slab=above),
        send(guess_ref.at[pl.ds(0, depth)], guess_after_ref, guess_send.at[1], guess_recv.at[1], slab=below),
    ]
    for copy in near:
        copy.wait_recv()
    mine = class_of(0)
    total = partial_ref[pl.ds(mine, CLASS_ROWS), :].astype(jnp.float32)
    for slot in range(NEAR_SLOTS):
        total = total + near_in[slot].astype(jnp.float32)
    near_sum[...] = total.astype(near_sum.dtype)

    far = [
        send(
            near_sum.at[pl.ds(piece_of(step, other), PIECE)], far_in.at[i],
            far_send.at[i], far_recv.at[i], rep=rep_of(4 * step, other),
        )
        for i, (step, other) in enumerate(FAR)
    ]
    for copy in far:
        copy.wait_recv()
    own = piece_of(0, 0)
    total = near_sum[pl.ds(own, PIECE), :].astype(jnp.float32)
    for i in range(len(FAR)):
        total = total + far_in[i].astype(jnp.float32)
    spot = pl.ds(pl.multiple_of(mine + own, PIECE), PIECE)
    charge_ref[spot, :] = total.astype(charge_ref.dtype)

    spreads = [
        send(
            charge_ref.at[spot], charge_ref.at[spot],
            spread_send.at[i], spread_recv.at[i], rep=rep_of(4 * step, other),
        )
        for i, (step, other) in enumerate(FAR)
    ]
    for copy in spreads:
        copy.wait_recv()
    lasts = []
    for i, (step, first, rows, _) in enumerate(NEAR):
        block = charge_ref.at[pl.ds(mine + first, rows)]
        lasts.append(send(block, block, last_send.at[i], last_recv.at[i], rep=rep_of(step)))

    def pass_on(i, start, rows):
        block = pl.ds(start, rows)
        target = jnp.where(start < middle, below, above)
        return send(charge_ref.at[block], halo_ref.at[block], halo_send.at[i], halo_recv.at[i], slab=target)

    halos = [pass_on(len(NEAR), mine, CLASS_ROWS)]
    for i in (2, 3, 0, 1):
        step, first, rows, _ = NEAR[i]
        lasts[i].wait_recv()
        halos.append(pass_on(i, class_of(-step) + first, rows))
    for copy in guesses + halos:
        copy.wait_recv()
    for copy in near + far + spreads + lasts + guesses + halos:
        copy.wait_send()


def solve_kernel(
    counts_ref,
    cells_ref,
    guess_ref,
    guess_before_ref,
    guess_after_ref,
    charge_ref,
    halo_ref,
    out_ref,
    even,
    odd,
    charge,
    table,
):
    planes, side, _ = guess_ref.shape
    depth = guess_before_ref.shape[0]
    total = cells_ref.shape[1]
    inside = pl.ds(PAD, side)

    blank = jnp.zeros((PAD, LANES), jnp.float32)

    @pl.loop(0, planes + 2 * depth)
    def _(plane):
        for buffer in (even, odd):
            buffer[plane, pl.ds(0, PAD), :] = blank
            buffer[plane, pl.ds(PAD + side, PAD), :] = blank

    @pl.loop(0, depth)
    def _(plane):
        even[plane, inside, :] = guess_before_ref[plane]
        even[depth + planes + plane, inside, :] = guess_after_ref[plane]

    @pl.loop(0, planes)
    def _(plane):
        even[depth + plane, inside, :] = guess_ref[plane]
        charge[depth - 1 + plane] = charge_ref[plane].astype(jnp.float32)

    @pl.loop(0, depth - 1)
    def _(plane):
        charge[plane] = halo_ref[depth - 1 + plane].astype(jnp.float32)
        charge[depth - 1 + planes + plane] = halo_ref[plane].astype(jnp.float32)

    lane = lax.broadcasted_iota(jnp.int32, (side, LANES), 1)
    first, last = lane == 0, lane == LANES - 1

    def beside(value):
        left = jnp.where(first, 0.0, pltpu.roll(value, 1, 1))
        right = jnp.where(last, 0.0, pltpu.roll(value, LANES - 1, 1))
        return left, right

    buffers = (even, odd)
    for sweep, (keep, previous, push) in enumerate(coefficients()):
        now, later = buffers[sweep % 2], buffers[(sweep + 1) % 2]

        @pl.loop(sweep + 1, planes + 2 * depth - 1 - sweep, unroll=2)
        def _(plane):
            value = now[plane, inside, :]
            left, right = beside(value)
            around = (left + right) + (
                now[plane, pl.ds(PAD - 1, side), :] + now[plane, pl.ds(PAD + 1, side), :]
            )
            around = around + (now[plane - 1, inside, :] + now[plane + 1, inside, :])
            fresh = keep * value + push * (charge[plane - 1] + around)
            if sweep:
                fresh = fresh - previous * later[plane, inside, :]
            later[plane, inside, :] = fresh

    final = buffers[SWEEPS % 2]
    for plane in range(planes):
        at = depth + plane
        spot = slice(plane * LANES, (plane + 1) * LANES)
        left, right = beside(final[at, inside, :])
        parts = (
            final[at, pl.ds(PAD - 1, side), :] - final[at, pl.ds(PAD + 1, side), :],
            left - right,
            final[at - 1, inside, :] - final[at + 1, inside, :],
        )
        for part, difference in enumerate(parts):
            table[part * side : (part + 1) * side, spot] = (difference * 0.5).astype(jnp.bfloat16)

    block = 256
    keys = lax.broadcasted_iota(jnp.int32, (planes * LANES, block), 0)
    ranks = lax.broadcasted_iota(jnp.int32, (side, block), 0)
    for start in range(0, total, block):
        cells = cells_ref[:, start : start + block]
        key = ((cells >> 14) << 7) | (cells & (LANES - 1))
        rank = (cells >> 7) & (LANES - 1)
        onehot = jnp.where(keys == key, 1.0, 0.0).astype(jnp.bfloat16)
        picked = jnp.dot(table[...], onehot, preferred_element_type=jnp.float32)
        slot = lax.broadcasted_iota(jnp.int32, (1, block), 1) + start
        live = slot < counts_ref[0, 0]
        chosen = (ranks == rank) & live
        for part in range(3):
            values = jnp.where(chosen, picked[part * side : (part + 1) * side], 0.0)
            out_ref[part, :, start : start + block] = KICK_STRENGTH * jnp.sum(
                values, axis=0, keepdims=True
            )


def local(cells, charges, counts, potential_guess):
    planes, side, _ = potential_guess.shape
    total = cells.shape[1]
    depth = SWEEPS + 1
    vmem = pl.BlockSpec(memory_space=pltpu.VMEM)
    smem = pl.BlockSpec(memory_space=pltpu.SMEM)
    params = pltpu.CompilerParams(vmem_limit_bytes=VMEM_LIMIT)

    rows = planes * side
    near = pltpu.SemaphoreType.DMA((len(NEAR),))
    far = pltpu.SemaphoreType.DMA((len(FAR),))
    halos = pltpu.SemaphoreType.DMA((len(NEAR) + 1,))
    pair = pltpu.SemaphoreType.DMA((2,))
    grid = jax.ShapeDtypeStruct((rows, LANES), jnp.bfloat16)
    ends = jax.ShapeDtypeStruct((depth, side, LANES), jnp.float32)
    charge, halo, guess_before, guess_after = pl.pallas_call(
        reduce_kernel,
        out_shape=[grid, grid, ends, ends],
        in_specs=[smem] + [vmem] * 3,
        out_specs=[vmem] * 4,
        scratch_shapes=[
            pltpu.VMEM((rows, LANES), jnp.bfloat16),
            pltpu.VMEM((NEAR_SLOTS, CLASS_ROWS, LANES), jnp.bfloat16),
            pltpu.VMEM((CLASS_ROWS, LANES), jnp.bfloat16),
            pltpu.VMEM((len(FAR), PIECE, LANES), jnp.bfloat16),
            near, near, far, far, far, far, near, near, halos, halos, pair, pair,
        ],
        compiler_params=pltpu.CompilerParams(
            vmem_limit_bytes=VMEM_LIMIT, collective_id=0, has_side_effects=True
        ),
    )(counts, cells, charges, potential_guess)
    charge = charge.reshape(planes, side, LANES)
    halo = halo.reshape(planes, side, LANES)
    deep = planes + 2 * depth
    kicks = pl.pallas_call(
        solve_kernel,
        out_shape=jax.ShapeDtypeStruct((3, 1, total), jnp.float32),
        in_specs=[smem] + [vmem] * 6,
        out_specs=vmem,
        scratch_shapes=[
            pltpu.VMEM((deep, side + 2 * PAD, LANES), jnp.float32),
            pltpu.VMEM((deep, side + 2 * PAD, LANES), jnp.float32),
            pltpu.VMEM((deep - 2, side, LANES), jnp.float32),
            pltpu.VMEM((3 * side, planes * LANES), jnp.bfloat16),
        ],
        compiler_params=params,
    )(counts, cells, potential_guess, guess_before, guess_after, charge, halo)
    return kicks


def solution(mesh):
    return jax.shard_map(
        local,
        mesh=mesh,
        in_specs=(P("slab", "rep"), P("slab", "rep"), P("slab", "rep"), P("slab", None, None)),
        out_specs=P(None, "slab", "rep"),
        check_vma=False,
    )
```

```python
import jax
import jax.numpy as jnp
from jax import lax
from jax.experimental import pallas as pl
from jax.experimental.pallas import tpu as pltpu
from jax.sharding import PartitionSpec as P

SWEEPS = 8
SCREEN_TERM = 0.05
KICK_STRENGTH = 1.0
DIAG = 6.0 + SCREEN_TERM
PAD = 8
LANES = 128
VMEM_LIMIT = 60 * 1024 * 1024


def coefficients():
    lower = SCREEN_TERM / DIAG
    upper = (12.0 + SCREEN_TERM) / DIAG
    centre = (upper + lower) / 2.0
    radius = (upper - lower) / 2.0
    sigma_ratio = centre / radius
    rho = 1.0 / sigma_ratio
    push = 1.0 / (DIAG * centre)
    result = [(0.0, push)]
    for _ in range(SWEEPS - 1):
        rho_next = 1.0 / (2.0 * sigma_ratio - rho)
        alpha = rho_next * rho
        push = 2.0 * rho_next / radius / DIAG
        result.append((alpha, push))
        rho = rho_next
    return result


def deposit(counts_ref, cells_ref, charges_ref, out_ref):
    total = cells_ref.shape[1]
    rows = out_ref.shape[0]
    cells = cells_ref[...]
    live = lax.broadcasted_iota(jnp.int32, (1, total), 1) < counts_ref[0, 0]
    weights = jnp.where(live, charges_ref[...].astype(jnp.float32), 0.0)
    column = cells & (LANES - 1)
    row = cells >> 7
    spread = jnp.where(
        lax.broadcasted_iota(jnp.int32, (LANES, total), 0) == column, weights, 0.0
    ).astype(jnp.bfloat16)
    block = 256
    iota = lax.broadcasted_iota(jnp.int32, (block, total), 0)
    for start in range(0, rows, block):
        onehot = jnp.where(iota == row - start, 1.0, 0.0).astype(jnp.bfloat16)
        out_ref[start : start + block, :] = lax.dot_general(
            onehot, spread, (((1,), (1,)), ((), ())), preferred_element_type=jnp.float32
        ).astype(out_ref.dtype)


CLASS_ROWS = 512
HALF = CLASS_ROWS // 2
NEAR = ((2, 0, HALF, 2), (-2, HALF, HALF, 2), (1, 0, CLASS_ROWS, 0), (-1, 0, CLASS_ROWS, 1))
NEAR_SLOTS = 3
FAR = ((2, 1), (2, 0), (1, 1), (3, 1), (1, 0), (3, 0), (0, 1))
PIECE = CLASS_ROWS // 8
MESH = pl.DeviceIdType.MESH


def reduce_kernel(
    counts_ref,
    cells_ref,
    charges_ref,
    guess_ref,
    charge_ref,
    halo_ref,
    guess_before_ref,
    guess_after_ref,
    partial_ref,
    near_in,
    near_sum,
    far_in,
    near_send,
    near_recv,
    far_send,
    far_recv,
    spread_send,
    spread_recv,
    last_send,
    last_recv,
    halo_send,
    halo_recv,
    guess_send,
    guess_recv,
):
    ring = lax.axis_size("rep") // 2
    rep = lax.axis_index("rep")
    z, x = rep // 2, lax.rem(rep, 2)
    slabs = lax.axis_size("slab")
    slab = lax.axis_index("slab")
    above, below = lax.rem(slab + 1, slabs), lax.rem(slab + slabs - 1, slabs)
    planes = guess_ref.shape[0]
    depth = guess_before_ref.shape[0]
    middle = charge_ref.shape[0] // 2

    def rep_of(step, other=0):
        return lax.rem(z + step + ring, ring) * 2 + (1 - x if other else x)

    def class_of(step):
        return pl.multiple_of(lax.rem(z + step + ring, 4) * CLASS_ROWS, CLASS_ROWS)

    def piece_of(step, other):
        lot = lax.rem(z // 4 + step, 4) * 2 + (1 - x if other else x)
        return pl.multiple_of(lot * PIECE, PIECE)

    def send(src, dst, send_sem, recv_sem, **target):
        copy = pltpu.make_async_remote_copy(
            src_ref=src, dst_ref=dst, send_sem=send_sem, recv_sem=recv_sem,
            device_id=target, device_id_type=MESH,
        )
        copy.start()
        return copy

    barrier = pltpu.get_barrier_semaphore()
    for step, other in FAR:
        pl.semaphore_signal(barrier, inc=1, device_id={"rep": rep_of(4 * step, other)}, device_id_type=MESH)
    for step, _, _, _ in NEAR:
        pl.semaphore_signal(barrier, inc=1, device_id={"rep": rep_of(step)}, device_id_type=MESH)
    for target in (above, below):
        pl.semaphore_signal(barrier, inc=1, device_id={"slab": target}, device_id_type=MESH)

    deposit(counts_ref, cells_ref, charges_ref, partial_ref)
    pl.semaphore_wait(barrier, len(FAR) + len(NEAR) + 2)

    near = [
        send(
            partial_ref.at[pl.ds(class_of(step) + first, rows)],
            near_in.at[slot, pl.ds(first, rows)],
            near_send.at[i], near_recv.at[i], rep=rep_of(step),
        )
        for i, (step, first, rows, slot) in enumerate(NEAR)
    ]
    guesses = [
        send(guess_ref.at[pl.ds(planes - depth, depth)], guess_before_ref, guess_send.at[0], guess_recv.at[0], slab=above),
        send(guess_ref.at[pl.ds(0, depth)], guess_after_ref, guess_send.at[1], guess_recv.at[1], slab=below),
    ]
    for copy in near:
        copy.wait_recv()
    mine = class_of(0)
    total = partial_ref[pl.ds(mine, CLASS_ROWS), :].astype(jnp.float32)
    for slot in range(NEAR_SLOTS):
        total = total + near_in[slot].astype(jnp.float32)
    near_sum[...] = total.astype(near_sum.dtype)

    far = [
        send(
            near_sum.at[pl.ds(piece_of(step, other), PIECE)], far_in.at[i],
            far_send.at[i], far_recv.at[i], rep=rep_of(4 * step, other),
        )
        for i, (step, other) in enumerate(FAR)
    ]
    for copy in far:
        copy.wait_recv()
    own = piece_of(0, 0)
    total = near_sum[pl.ds(own, PIECE), :].astype(jnp.float32)
    for i in range(len(FAR)):
        total = total + far_in[i].astype(jnp.float32)
    spot = pl.ds(pl.multiple_of(mine + own, PIECE), PIECE)
    charge_ref[spot, :] = total.astype(charge_ref.dtype)

    spreads = [
        send(
            charge_ref.at[spot], charge_ref.at[spot],
            spread_send.at[i], spread_recv.at[i], rep=rep_of(4 * step, other),
        )
        for i, (step, other) in enumerate(FAR)
    ]
    for copy in spreads:
        copy.wait_recv()
    lasts = []
    for i, (step, first, rows, _) in enumerate(NEAR):
        block = charge_ref.at[pl.ds(mine + first, rows)]
        lasts.append(send(block, block, last_send.at[i], last_recv.at[i], rep=rep_of(step)))

    def pass_on(i, start, rows):
        block = pl.ds(start, rows)
        target = jnp.where(start < middle, below, above)
        return send(charge_ref.at[block], halo_ref.at[block], halo_send.at[i], halo_recv.at[i], slab=target)

    halos = [pass_on(len(NEAR), mine, CLASS_ROWS)]
    for i in (2, 3, 0, 1):
        step, first, rows, _ = NEAR[i]
        lasts[i].wait_recv()
        halos.append(pass_on(i, class_of(-step) + first, rows))
    for copy in guesses + halos:
        copy.wait_recv()
    for copy in near + far + spreads + lasts + guesses + halos:
        copy.wait_send()


def solve_kernel(
    counts_ref,
    cells_ref,
    guess_ref,
    guess_before_ref,
    guess_after_ref,
    charge_ref,
    halo_ref,
    out_ref,
    even,
    odd,
    charge,
    table,
):
    planes, side, _ = guess_ref.shape
    depth = guess_before_ref.shape[0]
    total = cells_ref.shape[1]
    inside = pl.ds(PAD, side)

    blank = jnp.zeros((PAD, LANES), jnp.float32)

    @pl.loop(0, planes + 2 * depth)
    def _(plane):
        for buffer in (even, odd):
            buffer[plane, pl.ds(0, PAD), :] = blank
            buffer[plane, pl.ds(PAD + side, PAD), :] = blank

    @pl.loop(0, depth)
    def _(plane):
        even[plane, inside, :] = guess_before_ref[plane]
        even[depth + planes + plane, inside, :] = guess_after_ref[plane]

    @pl.loop(0, planes)
    def _(plane):
        even[depth + plane, inside, :] = guess_ref[plane]
        charge[depth - 1 + plane] = charge_ref[plane].astype(jnp.float32)

    @pl.loop(0, depth - 1)
    def _(plane):
        charge[plane] = halo_ref[depth - 1 + plane].astype(jnp.float32)
        charge[depth - 1 + planes + plane] = halo_ref[plane].astype(jnp.float32)

    def beside(value):
        lane = lax.broadcasted_iota(jnp.int32, value.shape, 1)
        first, last = lane == 0, lane == LANES - 1
        left = jnp.where(first, 0.0, pltpu.roll(value, 1, 1))
        right = jnp.where(last, 0.0, pltpu.roll(value, LANES - 1, 1))
        return left, right

    buffers = (even, odd)
    for sweep, (previous, push) in enumerate(coefficients()):
        now, later = buffers[sweep % 2], buffers[(sweep + 1) % 2]

        for start in range(0, side, 64):
            rows = pl.ds(PAD + start, 64)
            lower = now[sweep, rows, :]
            value = now[sweep + 1, rows, :]
            for plane in range(sweep + 1, planes + 2 * depth - 1 - sweep):
                upper = now[plane + 1, rows, :]
                left, right = beside(value)
                around = now[plane, pl.ds(PAD + start - 1, 64), :] + now[plane, pl.ds(PAD + start + 1, 64), :]
                around = around + (lower + upper)
                around = around + charge[plane - 1, pl.ds(start, 64), :]
                fresh = push * (around + (left + right))
                if sweep:
                    fresh = fresh - previous * later[plane, rows, :]
                later[plane, rows, :] = fresh
                lower, value = value, upper

    final = buffers[SWEEPS % 2]
    for plane in range(planes):
        at = depth + plane
        spot = slice(plane * LANES, (plane + 1) * LANES)
        left, right = beside(final[at, inside, :])
        parts = (
            final[at, pl.ds(PAD - 1, side), :] - final[at, pl.ds(PAD + 1, side), :],
            left - right,
            final[at - 1, inside, :] - final[at + 1, inside, :],
        )
        for part, difference in enumerate(parts):
            table[part * side : (part + 1) * side, spot] = (difference * 0.5).astype(jnp.bfloat16)

    block = 256
    keys = lax.broadcasted_iota(jnp.int32, (planes * LANES, block), 0)
    ranks = lax.broadcasted_iota(jnp.int32, (side, block), 0)
    for start in range(0, total, block):
        cells = cells_ref[:, start : start + block]
        key = ((cells >> 14) << 7) | (cells & (LANES - 1))
        rank = (cells >> 7) & (LANES - 1)
        onehot = jnp.where(keys == key, 1.0, 0.0).astype(jnp.bfloat16)
        picked = jnp.dot(table[...], onehot, preferred_element_type=jnp.float32)
        slot = lax.broadcasted_iota(jnp.int32, (1, block), 1) + start
        live = slot < counts_ref[0, 0]
        chosen = (ranks == rank) & live
        for part in range(3):
            values = jnp.where(chosen, picked[part * side : (part + 1) * side], 0.0)
            out_ref[part, :, start : start + block] = KICK_STRENGTH * jnp.sum(
                values, axis=0, keepdims=True
            )


def local(cells, charges, counts, potential_guess):
    planes, side, _ = potential_guess.shape
    total = cells.shape[1]
    depth = SWEEPS + 1
    vmem = pl.BlockSpec(memory_space=pltpu.VMEM)
    smem = pl.BlockSpec(memory_space=pltpu.SMEM)
    params = pltpu.CompilerParams(vmem_limit_bytes=VMEM_LIMIT)

    rows = planes * side
    near = pltpu.SemaphoreType.DMA((len(NEAR),))
    far = pltpu.SemaphoreType.DMA((len(FAR),))
    halos = pltpu.SemaphoreType.DMA((len(NEAR) + 1,))
    pair = pltpu.SemaphoreType.DMA((2,))
    grid = jax.ShapeDtypeStruct((rows, LANES), jnp.bfloat16)
    ends = jax.ShapeDtypeStruct((depth, side, LANES), jnp.float32)
    charge, halo, guess_before, guess_after = pl.pallas_call(
        reduce_kernel,
        out_shape=[grid, grid, ends, ends],
        in_specs=[smem] + [vmem] * 3,
        out_specs=[vmem] * 4,
        scratch_shapes=[
            pltpu.VMEM((rows, LANES), jnp.bfloat16),
            pltpu.VMEM((NEAR_SLOTS, CLASS_ROWS, LANES), jnp.bfloat16),
            pltpu.VMEM((CLASS_ROWS, LANES), jnp.bfloat16),
            pltpu.VMEM((len(FAR), PIECE, LANES), jnp.bfloat16),
            near, near, far, far, far, far, near, near, halos, halos, pair, pair,
        ],
        compiler_params=pltpu.CompilerParams(
            vmem_limit_bytes=VMEM_LIMIT, collective_id=0, has_side_effects=True
        ),
    )(counts, cells, charges, potential_guess)
    charge = charge.reshape(planes, side, LANES)
    halo = halo.reshape(planes, side, LANES)
    deep = planes + 2 * depth
    kicks = pl.pallas_call(
        solve_kernel,
        out_shape=jax.ShapeDtypeStruct((3, 1, total), jnp.float32),
        in_specs=[smem] + [vmem] * 6,
        out_specs=vmem,
        scratch_shapes=[
            pltpu.VMEM((deep, side + 2 * PAD, LANES), jnp.float32),
            pltpu.VMEM((deep, side + 2 * PAD, LANES), jnp.float32),
            pltpu.VMEM((deep - 2, side, LANES), jnp.float32),
            pltpu.VMEM((3 * side, planes * LANES), jnp.bfloat16),
        ],
        compiler_params=params,
    )(counts, cells, potential_guess, guess_before, guess_after, charge, halo)
    return kicks


def solution(mesh):
    return jax.shard_map(
        local,
        mesh=mesh,
        in_specs=(P("slab", "rep"), P("slab", "rep"), P("slab", "rep"), P("slab", None, None)),
        out_specs=P(None, "slab", "rep"),
        check_vma=False,
    )
```

```python
import jax
import jax.numpy as jnp
from jax import lax
from jax.experimental import pallas as pl
from jax.experimental.pallas import tpu as pltpu
from jax.sharding import PartitionSpec as P

SWEEPS = 8
SCREEN_TERM = 0.05
KICK_STRENGTH = 1.0
DIAG = 6.0 + SCREEN_TERM
PAD = 8
LANES = 128
VMEM_LIMIT = 60 * 1024 * 1024


def coefficients():
    lower = SCREEN_TERM / DIAG
    upper = (12.0 + SCREEN_TERM) / DIAG
    centre = (upper + lower) / 2.0
    radius = (upper - lower) / 2.0
    sigma_ratio = centre / radius
    rho = 1.0 / sigma_ratio
    push = 1.0 / (DIAG * centre)
    result = [(0.0, push)]
    for _ in range(SWEEPS - 1):
        rho_next = 1.0 / (2.0 * sigma_ratio - rho)
        alpha = rho_next * rho
        push = 2.0 * rho_next / radius / DIAG
        result.append((alpha, push))
        rho = rho_next
    return result


def deposit(counts_ref, cells_ref, charges_ref, out_ref):
    total = cells_ref.shape[1]
    rows = out_ref.shape[0]
    cells = cells_ref[...]
    live = lax.broadcasted_iota(jnp.int32, (1, total), 1) < counts_ref[0, 0]
    weights = jnp.where(live, charges_ref[...].astype(jnp.float32), 0.0)
    column = cells & (LANES - 1)
    row = cells >> 7
    spread = jnp.where(
        lax.broadcasted_iota(jnp.int32, (LANES, total), 0) == column, weights, 0.0
    ).astype(jnp.bfloat16)
    block = 256
    iota = lax.broadcasted_iota(jnp.int32, (block, total), 0)
    for start in range(0, rows, block):
        onehot = jnp.where(iota == row - start, 1.0, 0.0).astype(jnp.bfloat16)
        out_ref[start : start + block, :] = lax.dot_general(
            onehot, spread, (((1,), (1,)), ((), ())), preferred_element_type=jnp.float32
        ).astype(out_ref.dtype)


CLASS_ROWS = 256
HALF = CLASS_ROWS // 2
NEAR = (
    (2, 1, 0, HALF, 6),
    (-2, 1, HALF, HALF, 6),
    (1, 1, 0, CLASS_ROWS, 2),
    (-1, 1, 0, CLASS_ROWS, 4),
    (0, 1, 0, CLASS_ROWS, 0),
    (2, 0, 0, HALF, 5),
    (-2, 0, HALF, HALF, 5),
    (1, 0, 0, CLASS_ROWS, 1),
    (-1, 0, 0, CLASS_ROWS, 3),
)
NEAR_SLOTS = 7
ARRIVALS = (7, 8, 4, 5, 6, 2, 3, 0, 1)
FAR = (2, 1, 3)
PIECE = CLASS_ROWS // 4
MESH = pl.DeviceIdType.MESH


def reduce_kernel(
    counts_ref,
    cells_ref,
    charges_ref,
    guess_ref,
    charge_ref,
    halo_ref,
    guess_before_ref,
    guess_after_ref,
    partial_ref,
    near_in,
    near_sum,
    far_in,
    near_send,
    near_recv,
    far_send,
    far_recv,
    spread_send,
    spread_recv,
    last_send,
    last_recv,
    halo_send,
    halo_recv,
    guess_send,
    guess_recv,
):
    ring = lax.axis_size("rep") // 2
    rep = lax.axis_index("rep")
    z, x = rep // 2, lax.rem(rep, 2)
    slabs = lax.axis_size("slab")
    slab = lax.axis_index("slab")
    above, below = lax.rem(slab + 1, slabs), lax.rem(slab + slabs - 1, slabs)
    planes = guess_ref.shape[0]
    depth = guess_before_ref.shape[0]
    middle = charge_ref.shape[0] // 2

    def rep_of(step, other=0):
        return lax.rem(z + step + ring, ring) * 2 + (1 - x if other else x)

    def class_of(step, other=0):
        lot = lax.rem(z + step + ring, 4) * 2 + (1 - x if other else x)
        return pl.multiple_of(lot * CLASS_ROWS, CLASS_ROWS)

    def piece_of(step):
        return pl.multiple_of(lax.rem(z // 4 + step, 4) * PIECE, PIECE)

    def send(src, dst, send_sem, recv_sem, **target):
        copy = pltpu.make_async_remote_copy(
            src_ref=src, dst_ref=dst, send_sem=send_sem, recv_sem=recv_sem,
            device_id=target, device_id_type=MESH,
        )
        copy.start()
        return copy

    barrier = pltpu.get_barrier_semaphore()
    for step in FAR:
        pl.semaphore_signal(barrier, inc=1, device_id={"rep": rep_of(4 * step)}, device_id_type=MESH)
    for step, other, _, _, _ in NEAR:
        pl.semaphore_signal(barrier, inc=1, device_id={"rep": rep_of(step, other)}, device_id_type=MESH)
    for target in (above, below):
        pl.semaphore_signal(barrier, inc=1, device_id={"slab": target}, device_id_type=MESH)

    deposit(counts_ref, cells_ref, charges_ref, partial_ref)
    pl.semaphore_wait(barrier, len(FAR) + len(NEAR) + 2)

    near = [
        send(
            partial_ref.at[pl.ds(class_of(step, other) + first, rows)],
            near_in.at[slot, pl.ds(first, rows)],
            near_send.at[i], near_recv.at[i], rep=rep_of(step, other),
        )
        for i, (step, other, first, rows, slot) in enumerate(NEAR)
    ]
    for copy in near:
        copy.wait_recv()
    mine = class_of(0)
    total = partial_ref[pl.ds(mine, CLASS_ROWS), :].astype(jnp.float32)
    for slot in range(NEAR_SLOTS):
        total = total + near_in[slot].astype(jnp.float32)
    near_sum[...] = total.astype(near_sum.dtype)

    far = [
        send(
            near_sum.at[pl.ds(piece_of(step), PIECE)], far_in.at[i],
            far_send.at[i], far_recv.at[i], rep=rep_of(4 * step),
        )
        for i, step in enumerate(FAR)
    ]
    guesses = [
        send(guess_ref.at[pl.ds(planes - depth, depth)], guess_before_ref, guess_send.at[0], guess_recv.at[0], slab=above),
        send(guess_ref.at[pl.ds(0, depth)], guess_after_ref, guess_send.at[1], guess_recv.at[1], slab=below),
    ]
    for copy in far:
        copy.wait_recv()
    own = piece_of(0)
    total = near_sum[pl.ds(own, PIECE), :].astype(jnp.float32)
    for i in range(len(FAR)):
        total = total + far_in[i].astype(jnp.float32)
    spot = pl.ds(pl.multiple_of(mine + own, PIECE), PIECE)
    charge_ref[spot, :] = total.astype(charge_ref.dtype)

    spreads = [
        send(
            charge_ref.at[spot], charge_ref.at[spot],
            spread_send.at[i], spread_recv.at[i], rep=rep_of(4 * step),
        )
        for i, step in enumerate(FAR)
    ]
    for copy in spreads:
        copy.wait_recv()
    lasts = []
    for i, (step, other, first, rows, _) in enumerate(NEAR):
        block = charge_ref.at[pl.ds(mine + first, rows)]
        lasts.append(send(block, block, last_send.at[i], last_recv.at[i], rep=rep_of(step, other)))

    def pass_on(i, start, rows):
        block = pl.ds(start, rows)
        target = jnp.where(start < middle, below, above)
        return send(charge_ref.at[block], halo_ref.at[block], halo_send.at[i], halo_recv.at[i], slab=target)

    halos = [pass_on(len(NEAR), mine, CLASS_ROWS)]
    for i in ARRIVALS:
        step, other, first, rows, _ = NEAR[i]
        lasts[i].wait_recv()
        halos.append(pass_on(i, class_of(-step, other) + first, rows))
    for copy in guesses + halos:
        copy.wait_recv()
    for copy in near + far + spreads + lasts + guesses + halos:
        copy.wait_send()


def solve_kernel(
    counts_ref,
    cells_ref,
    guess_ref,
    guess_before_ref,
    guess_after_ref,
    charge_ref,
    halo_ref,
    out_ref,
    even,
    odd,
    charge,
    table,
):
    planes, side, _ = guess_ref.shape
    depth = guess_before_ref.shape[0]
    total = cells_ref.shape[1]
    inside = pl.ds(PAD, side)

    blank = jnp.zeros((PAD, LANES), jnp.float32)

    @pl.loop(0, planes + 2 * depth)
    def _(plane):
        for buffer in (even, odd):
            buffer[plane, pl.ds(0, PAD), :] = blank
            buffer[plane, pl.ds(PAD + side, PAD), :] = blank

    @pl.loop(0, depth)
    def _(plane):
        even[plane, inside, :] = guess_before_ref[plane]
        even[depth + planes + plane, inside, :] = guess_after_ref[plane]

    @pl.loop(0, planes)
    def _(plane):
        even[depth + plane, inside, :] = guess_ref[plane]
        charge[depth - 1 + plane] = charge_ref[plane].astype(jnp.float32)

    @pl.loop(0, depth - 1)
    def _(plane):
        charge[plane] = halo_ref[depth - 1 + plane].astype(jnp.float32)
        charge[depth - 1 + planes + plane] = halo_ref[plane].astype(jnp.float32)

    def beside(value):
        lane = lax.broadcasted_iota(jnp.int32, value.shape, 1)
        first, last = lane == 0, lane == LANES - 1
        left = jnp.where(first, 0.0, pltpu.roll(value, 1, 1))
        right = jnp.where(last, 0.0, pltpu.roll(value, LANES - 1, 1))
        return left, right

    buffers = (even, odd)
    for sweep, (previous, push) in enumerate(coefficients()):
        now, later = buffers[sweep % 2], buffers[(sweep + 1) % 2]

        for start in range(0, side, 64):
            rows = pl.ds(PAD + start, 64)
            lower = now[sweep, rows, :]
            value = now[sweep + 1, rows, :]
            for plane in range(sweep + 1, planes + 2 * depth - 1 - sweep):
                upper = now[plane + 1, rows, :]
                left, right = beside(value)
                around = now[plane, pl.ds(PAD + start - 1, 64), :] + now[plane, pl.ds(PAD + start + 1, 64), :]
                around = around + (lower + upper)
                around = around + charge[plane - 1, pl.ds(start, 64), :]
                fresh = push * (around + (left + right))
                if sweep:
                    fresh = fresh - previous * later[plane, rows, :]
                later[plane, rows, :] = fresh
                lower, value = value, upper

    final = buffers[SWEEPS % 2]
    for plane in range(planes):
        at = depth + plane
        spot = slice(plane * LANES, (plane + 1) * LANES)
        left, right = beside(final[at, inside, :])
        parts = (
            final[at, pl.ds(PAD - 1, side), :] - final[at, pl.ds(PAD + 1, side), :],
            left - right,
            final[at - 1, inside, :] - final[at + 1, inside, :],
        )
        for part, difference in enumerate(parts):
            table[part * side : (part + 1) * side, spot] = (difference * 0.5).astype(jnp.bfloat16)

    block = 256
    keys = lax.broadcasted_iota(jnp.int16, (planes * LANES, block), 0)
    ranks = lax.broadcasted_iota(jnp.int32, (side, block), 0)
    for start in range(0, total, block):
        cells = cells_ref[:, start : start + block]
        key = ((cells >> 14) << 7) | (cells & (LANES - 1))
        rank = (cells >> 7) & (LANES - 1)
        onehot = jnp.where(keys == key.astype(jnp.int16), jnp.bfloat16(1.0), jnp.bfloat16(0.0))
        picked = jnp.dot(table[...], onehot, preferred_element_type=jnp.float32)
        slot = lax.broadcasted_iota(jnp.int32, (1, block), 1) + start
        live = slot < counts_ref[0, 0]
        chosen = (ranks == rank) & live
        for part in range(3):
            values = jnp.where(chosen, picked[part * side : (part + 1) * side], 0.0)
            out_ref[part, :, start : start + block] = KICK_STRENGTH * jnp.sum(
                values, axis=0, keepdims=True
            )


def local(cells, charges, counts, potential_guess):
    planes, side, _ = potential_guess.shape
    total = cells.shape[1]
    depth = SWEEPS + 1
    vmem = pl.BlockSpec(memory_space=pltpu.VMEM)
    smem = pl.BlockSpec(memory_space=pltpu.SMEM)
    params = pltpu.CompilerParams(vmem_limit_bytes=VMEM_LIMIT)

    rows = planes * side
    near = pltpu.SemaphoreType.DMA((len(NEAR),))
    far = pltpu.SemaphoreType.DMA((len(FAR),))
    halos = pltpu.SemaphoreType.DMA((len(NEAR) + 1,))
    pair = pltpu.SemaphoreType.DMA((2,))
    grid = jax.ShapeDtypeStruct((rows, LANES), jnp.bfloat16)
    ends = jax.ShapeDtypeStruct((depth, side, LANES), jnp.float32)
    charge, halo, guess_before, guess_after = pl.pallas_call(
        reduce_kernel,
        out_shape=[grid, grid, ends, ends],
        in_specs=[smem] + [vmem] * 3,
        out_specs=[vmem] * 4,
        scratch_shapes=[
            pltpu.VMEM((rows, LANES), jnp.bfloat16),
            pltpu.VMEM((NEAR_SLOTS, CLASS_ROWS, LANES), jnp.bfloat16),
            pltpu.VMEM((CLASS_ROWS, LANES), jnp.bfloat16),
            pltpu.VMEM((len(FAR), PIECE, LANES), jnp.bfloat16),
            near, near, far, far, far, far, near, near, halos, halos, pair, pair,
        ],
        compiler_params=pltpu.CompilerParams(
            vmem_limit_bytes=VMEM_LIMIT, collective_id=0, has_side_effects=True
        ),
    )(counts, cells, charges, potential_guess)
    charge = charge.reshape(planes, side, LANES)
    halo = halo.reshape(planes, side, LANES)
    deep = planes + 2 * depth
    kicks = pl.pallas_call(
        solve_kernel,
        out_shape=jax.ShapeDtypeStruct((3, 1, total), jnp.float32),
        in_specs=[smem] + [vmem] * 6,
        out_specs=vmem,
        scratch_shapes=[
            pltpu.VMEM((deep, side + 2 * PAD, LANES), jnp.float32),
            pltpu.VMEM((deep, side + 2 * PAD, LANES), jnp.float32),
            pltpu.VMEM((deep - 2, side, LANES), jnp.float32),
            pltpu.VMEM((3 * side, planes * LANES), jnp.bfloat16),
        ],
        compiler_params=params,
    )(counts, cells, potential_guess, guess_before, guess_after, charge, halo)
    return kicks


def solution(mesh):
    return jax.shard_map(
        local,
        mesh=mesh,
        in_specs=(P("slab", "rep"), P("slab", "rep"), P("slab", "rep"), P("slab", None, None)),
        out_specs=P(None, "slab", "rep"),
        check_vma=False,
    )
```

```python
import jax
import jax.numpy as jnp
from jax import lax
from jax.experimental import pallas as pl
from jax.experimental.pallas import tpu as pltpu
from jax.sharding import PartitionSpec as P

SWEEPS = 8
SCREEN_TERM = 0.05
KICK_STRENGTH = 1.0
DIAG = 6.0 + SCREEN_TERM
PAD = 8
LANES = 128
VMEM_LIMIT = 60 * 1024 * 1024


def coefficients():
    lower = SCREEN_TERM / DIAG
    upper = (12.0 + SCREEN_TERM) / DIAG
    centre = (upper + lower) / 2.0
    radius = (upper - lower) / 2.0
    sigma_ratio = centre / radius
    rho = 1.0 / sigma_ratio
    push = 1.0 / (DIAG * centre)
    result = [(0.0, push)]
    for _ in range(SWEEPS - 1):
        rho_next = 1.0 / (2.0 * sigma_ratio - rho)
        alpha = rho_next * rho
        push = 2.0 * rho_next / radius / DIAG
        result.append((alpha, push))
        rho = rho_next
    return result


def deposit(counts_ref, cells_ref, charges_ref, out_ref):
    total = cells_ref.shape[1]
    rows = out_ref.shape[0]
    cells = cells_ref[...]
    live = lax.broadcasted_iota(jnp.int32, (1, total), 1) < counts_ref[0, 0]
    weights = jnp.where(live, charges_ref[...].astype(jnp.float32), 0.0)
    column = cells & (LANES - 1)
    row = cells >> 7
    spread = jnp.where(
        lax.broadcasted_iota(jnp.int32, (LANES, total), 0) == column, weights, 0.0
    ).astype(jnp.bfloat16)
    block = 256
    iota = lax.broadcasted_iota(jnp.int32, (block, total), 0)
    for start in range(0, rows, block):
        onehot = jnp.where(iota == row - start, 1.0, 0.0).astype(jnp.bfloat16)
        out_ref[start : start + block, :] = lax.dot_general(
            onehot, spread, (((1,), (1,)), ((), ())), preferred_element_type=jnp.float32
        ).astype(out_ref.dtype)


CLASS_ROWS = 256
HALF = CLASS_ROWS // 2
NEAR = (
    (2, 1, 0, HALF, 6),
    (-2, 1, HALF, HALF, 6),
    (1, 1, 0, CLASS_ROWS, 2),
    (-1, 1, 0, CLASS_ROWS, 4),
    (0, 1, 0, CLASS_ROWS, 0),
    (2, 0, 0, HALF, 5),
    (-2, 0, HALF, HALF, 5),
    (1, 0, 0, CLASS_ROWS, 1),
    (-1, 0, 0, CLASS_ROWS, 3),
)
NEAR_SLOTS = 7
SHARE = ((1, 0), (-1, 0), (0, 1), (2, 0), (1, 1), (-1, 1), (2, 1))
FAR = (2, 1, 3)
PIECE = CLASS_ROWS // 4
MESH = pl.DeviceIdType.MESH


def reduce_kernel(
    counts_ref,
    cells_ref,
    charges_ref,
    guess_ref,
    charge_ref,
    halo_ref,
    guess_before_ref,
    guess_after_ref,
    partial_ref,
    near_in,
    near_sum,
    far_in,
    near_send,
    near_recv,
    far_send,
    far_recv,
    spread_send,
    spread_recv,
    last_send,
    last_recv,
    halo_send,
    halo_recv,
    guess_send,
    guess_recv,
):
    ring = lax.axis_size("rep") // 2
    rep = lax.axis_index("rep")
    z, x = rep // 2, lax.rem(rep, 2)
    slabs = lax.axis_size("slab")
    slab = lax.axis_index("slab")
    above, below = lax.rem(slab + 1, slabs), lax.rem(slab + slabs - 1, slabs)
    planes = guess_ref.shape[0]
    depth = guess_before_ref.shape[0]
    middle = charge_ref.shape[0] // 2

    def rep_of(step, other=0):
        return lax.rem(z + step + ring, ring) * 2 + (1 - x if other else x)

    def class_of(step, other=0):
        lot = lax.rem(z + step + ring, 4) * 2 + (1 - x if other else x)
        return pl.multiple_of(lot * CLASS_ROWS, CLASS_ROWS)

    def piece_of(step):
        return pl.multiple_of(lax.rem(z // 4 + step, 4) * PIECE, PIECE)

    def send(src, dst, send_sem, recv_sem, **target):
        copy = pltpu.make_async_remote_copy(
            src_ref=src, dst_ref=dst, send_sem=send_sem, recv_sem=recv_sem,
            device_id=target, device_id_type=MESH,
        )
        copy.start()
        return copy

    barrier = pltpu.get_barrier_semaphore()
    for step in FAR:
        pl.semaphore_signal(barrier, inc=1, device_id={"rep": rep_of(4 * step)}, device_id_type=MESH)
    for step, other, _, _, _ in NEAR:
        pl.semaphore_signal(barrier, inc=1, device_id={"rep": rep_of(step, other)}, device_id_type=MESH)
    for target in (above, below):
        pl.semaphore_signal(barrier, inc=1, device_id={"slab": target}, device_id_type=MESH)

    deposit(counts_ref, cells_ref, charges_ref, partial_ref)
    pl.semaphore_wait(barrier, len(FAR) + len(NEAR) + 2)

    near = [
        send(
            partial_ref.at[pl.ds(class_of(step, other) + first, rows)],
            near_in.at[slot, pl.ds(first, rows)],
            near_send.at[i], near_recv.at[i], rep=rep_of(step, other),
        )
        for i, (step, other, first, rows, slot) in enumerate(NEAR)
    ]
    for copy in near:
        copy.wait_recv()
    mine = class_of(0)
    total = partial_ref[pl.ds(mine, CLASS_ROWS), :].astype(jnp.float32)
    for slot in range(NEAR_SLOTS):
        total = total + near_in[slot].astype(jnp.float32)
    near_sum[...] = total.astype(near_sum.dtype)

    far = [
        send(
            near_sum.at[pl.ds(piece_of(step), PIECE)], far_in.at[i],
            far_send.at[i], far_recv.at[i], rep=rep_of(4 * step),
        )
        for i, step in enumerate(FAR)
    ]
    guesses = [
        send(guess_ref.at[pl.ds(planes - depth, depth)], guess_before_ref, guess_send.at[0], guess_recv.at[0], slab=above),
        send(guess_ref.at[pl.ds(0, depth)], guess_after_ref, guess_send.at[1], guess_recv.at[1], slab=below),
    ]
    for copy in far:
        copy.wait_recv()
    own = piece_of(0)
    total = near_sum[pl.ds(own, PIECE), :].astype(jnp.float32)
    for i in range(len(FAR)):
        total = total + far_in[i].astype(jnp.float32)
    spot = pl.ds(pl.multiple_of(mine + own, PIECE), PIECE)
    charge_ref[spot, :] = total.astype(charge_ref.dtype)

    spreads = [
        send(
            charge_ref.at[spot], charge_ref.at[spot],
            spread_send.at[i], spread_recv.at[i], rep=rep_of(4 * step),
        )
        for i, step in enumerate(FAR)
    ]
    def share(piece, order):
        block = charge_ref.at[pl.ds(pl.multiple_of(mine + piece * PIECE, PIECE), PIECE)]
        for i in reversed(range(len(SHARE))):
            step, other = SHARE[i]
            if step == 2:
                step = jnp.where(piece < 2, 2, -2)
            lasts[i].append(
                send(block, block, last_send.at[i, order], last_recv.at[i, piece], rep=rep_of(step, other))
            )

    def pass_on(i, start):
        block = pl.ds(start, CLASS_ROWS)
        target = jnp.where(start < middle, below, above)
        return send(charge_ref.at[block], halo_ref.at[block], halo_send.at[i], halo_recv.at[i], slab=target)

    lasts = [[] for _ in SHARE]
    lot = z // 4
    share(lot, 0)
    for order, i in enumerate((1, 2, 0)):
        spreads[i].wait_recv()
        share(lax.rem(lot + 4 - FAR[i], 4), order + 1)
    halos = [pass_on(len(SHARE), mine)]
    for i, (step, other) in enumerate(SHARE):
        for copy in lasts[i]:
            copy.wait_recv()
        halos.append(pass_on(i, class_of(-step, other)))
    lasts = [copy for copies in lasts for copy in copies]
    for copy in guesses + halos:
        copy.wait_recv()
    for copy in near + far + spreads + lasts + guesses + halos:
        copy.wait_send()


def solve_kernel(
    counts_ref,
    cells_ref,
    guess_ref,
    guess_before_ref,
    guess_after_ref,
    charge_ref,
    halo_ref,
    out_ref,
    even,
    odd,
    charge,
    table,
):
    planes, side, _ = guess_ref.shape
    depth = guess_before_ref.shape[0]
    total = cells_ref.shape[1]
    inside = pl.ds(PAD, side)

    blank = jnp.zeros((PAD, LANES), jnp.float32)

    @pl.loop(0, planes + 2 * depth)
    def _(plane):
        for buffer in (even, odd):
            buffer[plane, pl.ds(0, PAD), :] = blank
            buffer[plane, pl.ds(PAD + side, PAD), :] = blank

    @pl.loop(0, depth)
    def _(plane):
        even[plane, inside, :] = guess_before_ref[plane]
        even[depth + planes + plane, inside, :] = guess_after_ref[plane]

    @pl.loop(0, planes)
    def _(plane):
        even[depth + plane, inside, :] = guess_ref[plane]
        charge[depth - 1 + plane] = charge_ref[plane].astype(jnp.float32)

    @pl.loop(0, depth - 1)
    def _(plane):
        charge[plane] = halo_ref[depth - 1 + plane].astype(jnp.float32)
        charge[depth - 1 + planes + plane] = halo_ref[plane].astype(jnp.float32)

    def beside(value):
        lane = lax.broadcasted_iota(jnp.int32, value.shape, 1)
        first, last = lane == 0, lane == LANES - 1
        left = jnp.where(first, 0.0, pltpu.roll(value, 1, 1))
        right = jnp.where(last, 0.0, pltpu.roll(value, LANES - 1, 1))
        return left, right

    buffers = (even, odd)
    for sweep, (previous, push) in enumerate(coefficients()):
        now, later = buffers[sweep % 2], buffers[(sweep + 1) % 2]

        for start in range(0, side, 64):
            rows = pl.ds(PAD + start, 64)
            lower = now[sweep, rows, :]
            value = now[sweep + 1, rows, :]
            for plane in range(sweep + 1, planes + 2 * depth - 1 - sweep):
                upper = now[plane + 1, rows, :]
                left, right = beside(value)
                around = now[plane, pl.ds(PAD + start - 1, 64), :] + now[plane, pl.ds(PAD + start + 1, 64), :]
                around = around + (lower + upper)
                around = around + charge[plane - 1, pl.ds(start, 64), :]
                fresh = push * (around + (left + right))
                if sweep:
                    fresh = fresh - previous * later[plane, rows, :]
                later[plane, rows, :] = fresh
                lower, value = value, upper

    final = buffers[SWEEPS % 2]
    for plane in range(planes):
        at = depth + plane
        spot = slice(plane * LANES, (plane + 1) * LANES)
        left, right = beside(final[at, inside, :])
        parts = (
            final[at, pl.ds(PAD - 1, side), :] - final[at, pl.ds(PAD + 1, side), :],
            left - right,
            final[at - 1, inside, :] - final[at + 1, inside, :],
        )
        for part, difference in enumerate(parts):
            table[part * side : (part + 1) * side, spot] = (difference * 0.5).astype(jnp.bfloat16)

    block = 256
    keys = lax.broadcasted_iota(jnp.int16, (planes * LANES, block), 0)
    ranks = lax.broadcasted_iota(jnp.int32, (side, block), 0)
    for start in range(0, total, block):
        cells = cells_ref[:, start : start + block]
        key = ((cells >> 14) << 7) | (cells & (LANES - 1))
        rank = (cells >> 7) & (LANES - 1)
        onehot = jnp.where(keys == key.astype(jnp.int16), jnp.bfloat16(1.0), jnp.bfloat16(0.0))
        picked = jnp.dot(table[...], onehot, preferred_element_type=jnp.float32)
        slot = lax.broadcasted_iota(jnp.int32, (1, block), 1) + start
        live = slot < counts_ref[0, 0]
        chosen = (ranks == rank) & live
        for part in range(3):
            values = jnp.where(chosen, picked[part * side : (part + 1) * side], 0.0)
            out_ref[part, :, start : start + block] = KICK_STRENGTH * jnp.sum(
                values, axis=0, keepdims=True
            )


def local(cells, charges, counts, potential_guess):
    planes, side, _ = potential_guess.shape
    total = cells.shape[1]
    depth = SWEEPS + 1
    vmem = pl.BlockSpec(memory_space=pltpu.VMEM)
    smem = pl.BlockSpec(memory_space=pltpu.SMEM)
    params = pltpu.CompilerParams(vmem_limit_bytes=VMEM_LIMIT)

    rows = planes * side
    near = pltpu.SemaphoreType.DMA((len(NEAR),))
    far = pltpu.SemaphoreType.DMA((len(FAR),))
    share = pltpu.SemaphoreType.DMA((len(SHARE), 4))
    halos = pltpu.SemaphoreType.DMA((len(SHARE) + 1,))
    pair = pltpu.SemaphoreType.DMA((2,))
    grid = jax.ShapeDtypeStruct((rows, LANES), jnp.bfloat16)
    ends = jax.ShapeDtypeStruct((depth, side, LANES), jnp.float32)
    charge, halo, guess_before, guess_after = pl.pallas_call(
        reduce_kernel,
        out_shape=[grid, grid, ends, ends],
        in_specs=[smem] + [vmem] * 3,
        out_specs=[vmem] * 4,
        scratch_shapes=[
            pltpu.VMEM((rows, LANES), jnp.bfloat16),
            pltpu.VMEM((NEAR_SLOTS, CLASS_ROWS, LANES), jnp.bfloat16),
            pltpu.VMEM((CLASS_ROWS, LANES), jnp.bfloat16),
            pltpu.VMEM((len(FAR), PIECE, LANES), jnp.bfloat16),
            near, near, far, far, far, far, share, share, halos, halos, pair, pair,
        ],
        compiler_params=pltpu.CompilerParams(
            vmem_limit_bytes=VMEM_LIMIT, collective_id=0, has_side_effects=True
        ),
    )(counts, cells, charges, potential_guess)
    charge = charge.reshape(planes, side, LANES)
    halo = halo.reshape(planes, side, LANES)
    deep = planes + 2 * depth
    kicks = pl.pallas_call(
        solve_kernel,
        out_shape=jax.ShapeDtypeStruct((3, 1, total), jnp.float32),
        in_specs=[smem] + [vmem] * 6,
        out_specs=vmem,
        scratch_shapes=[
            pltpu.VMEM((deep, side + 2 * PAD, LANES), jnp.float32),
            pltpu.VMEM((deep, side + 2 * PAD, LANES), jnp.float32),
            pltpu.VMEM((deep - 2, side, LANES), jnp.float32),
            pltpu.VMEM((3 * side, planes * LANES), jnp.bfloat16),
        ],
        compiler_params=params,
    )(counts, cells, potential_guess, guess_before, guess_after, charge, halo)
    return kicks


def solution(mesh):
    return jax.shard_map(
        local,
        mesh=mesh,
        in_specs=(P("slab", "rep"), P("slab", "rep"), P("slab", "rep"), P("slab", None, None)),
        out_specs=P(None, "slab", "rep"),
        check_vma=False,
    )
```

```python
import jax
import jax.numpy as jnp
from jax import lax
from jax.experimental import pallas as pl
from jax.experimental.pallas import tpu as pltpu
from jax.sharding import PartitionSpec as P

SWEEPS = 8
SCREEN_TERM = 0.05
KICK_STRENGTH = 1.0
DIAG = 6.0 + SCREEN_TERM
PAD = 8
LANES = 128
VMEM_LIMIT = 60 * 1024 * 1024


def coefficients():
    lower = SCREEN_TERM / DIAG
    upper = (12.0 + SCREEN_TERM) / DIAG
    centre = (upper + lower) / 2.0
    radius = (upper - lower) / 2.0
    sigma_ratio = centre / radius
    rho = 1.0 / sigma_ratio
    push = 1.0 / (DIAG * centre)
    result = [(0.0, push)]
    for _ in range(SWEEPS - 1):
        rho_next = 1.0 / (2.0 * sigma_ratio - rho)
        alpha = rho_next * rho
        push = 2.0 * rho_next / radius / DIAG
        result.append((alpha, push))
        rho = rho_next
    return result


def deposit(counts_ref, cells_ref, charges_ref, out_ref):
    total = cells_ref.shape[1]
    rows = out_ref.shape[0]
    cells = cells_ref[...]
    live = lax.broadcasted_iota(jnp.int32, (1, total), 1) < counts_ref[0, 0]
    weights = jnp.where(live, charges_ref[...].astype(jnp.float32), 0.0)
    column = cells & (LANES - 1)
    row = cells >> 7
    spread = jnp.where(
        lax.broadcasted_iota(jnp.int32, (LANES, total), 0) == column, weights, 0.0
    ).astype(jnp.bfloat16)
    block = 256
    iota = lax.broadcasted_iota(jnp.int32, (block, total), 0)
    for start in range(0, rows, block):
        onehot = jnp.where(iota == row - start, 1.0, 0.0).astype(jnp.bfloat16)
        out_ref[start : start + block, :] = lax.dot_general(
            onehot, spread, (((1,), (1,)), ((), ())), preferred_element_type=jnp.float32
        ).astype(out_ref.dtype)


CLASS_ROWS = 256
HALF = CLASS_ROWS // 2
NEAR = (
    (2, 1, 0, HALF, 6),
    (-2, 1, HALF, HALF, 6),
    (1, 1, 0, CLASS_ROWS, 2),
    (-1, 1, 0, CLASS_ROWS, 4),
    (0, 1, 0, CLASS_ROWS, 0),
    (2, 0, 0, HALF, 5),
    (-2, 0, HALF, HALF, 5),
    (1, 0, 0, CLASS_ROWS, 1),
    (-1, 0, 0, CLASS_ROWS, 3),
)
NEAR_SLOTS = 7
ARRIVALS = (7, 8, 4, 5, 6, 2, 3, 0, 1)
FAR = (2, 1, 3)
PIECE = CLASS_ROWS // 4
MESH = pl.DeviceIdType.MESH


def reduce_kernel(
    counts_ref,
    cells_ref,
    charges_ref,
    guess_ref,
    charge_ref,
    halo_ref,
    guess_before_ref,
    guess_after_ref,
    partial_ref,
    near_in,
    near_sum,
    far_in,
    near_send,
    near_recv,
    far_send,
    far_recv,
    spread_send,
    spread_recv,
    last_send,
    last_recv,
    halo_send,
    halo_recv,
    guess_send,
    guess_recv,
):
    ring = lax.axis_size("rep") // 2
    rep = lax.axis_index("rep")
    z, x = rep // 2, lax.rem(rep, 2)
    slabs = lax.axis_size("slab")
    slab = lax.axis_index("slab")
    above, below = lax.rem(slab + 1, slabs), lax.rem(slab + slabs - 1, slabs)
    planes = guess_ref.shape[0]
    depth = guess_before_ref.shape[0]
    middle = charge_ref.shape[0] // 2

    def rep_of(step, other=0):
        return lax.rem(z + step + ring, ring) * 2 + (1 - x if other else x)

    def class_of(step, other=0):
        lot = lax.rem(z + step + ring, 4) * 2 + (1 - x if other else x)
        return pl.multiple_of(lot * CLASS_ROWS, CLASS_ROWS)

    def piece_of(step):
        return pl.multiple_of(lax.rem(z // 4 + step, 4) * PIECE, PIECE)

    def send(src, dst, send_sem, recv_sem, **target):
        copy = pltpu.make_async_remote_copy(
            src_ref=src, dst_ref=dst, send_sem=send_sem, recv_sem=recv_sem,
            device_id=target, device_id_type=MESH,
        )
        copy.start()
        return copy

    barrier = pltpu.get_barrier_semaphore()
    for step in FAR:
        pl.semaphore_signal(barrier, inc=1, device_id={"rep": rep_of(4 * step)}, device_id_type=MESH)
    for step, other, _, _, _ in NEAR:
        pl.semaphore_signal(barrier, inc=1, device_id={"rep": rep_of(step, other)}, device_id_type=MESH)
    for target in (above, below):
        pl.semaphore_signal(barrier, inc=1, device_id={"slab": target}, device_id_type=MESH)

    deposit(counts_ref, cells_ref, charges_ref, partial_ref)
    pl.semaphore_wait(barrier, len(FAR) + len(NEAR) + 2)

    near = [
        send(
            partial_ref.at[pl.ds(class_of(step, other) + first, rows)],
            near_in.at[slot, pl.ds(first, rows)],
            near_send.at[i], near_recv.at[i], rep=rep_of(step, other),
        )
        for i, (step, other, first, rows, slot) in enumerate(NEAR)
    ]
    for copy in near:
        copy.wait_recv()
    mine = class_of(0)
    total = partial_ref[pl.ds(mine, CLASS_ROWS), :].astype(jnp.float32)
    for slot in range(NEAR_SLOTS):
        total = total + near_in[slot].astype(jnp.float32)
    near_sum[...] = total.astype(near_sum.dtype)

    far = [
        send(
            near_sum.at[pl.ds(piece_of(step), PIECE)], far_in.at[i],
            far_send.at[i], far_recv.at[i], rep=rep_of(4 * step),
        )
        for i, step in enumerate(FAR)
    ]
    guesses = [
        send(guess_ref.at[pl.ds(planes - depth, depth)], guess_before_ref, guess_send.at[0], guess_recv.at[0], slab=above),
        send(guess_ref.at[pl.ds(0, depth)], guess_after_ref, guess_send.at[1], guess_recv.at[1], slab=below),
    ]
    for copy in far:
        copy.wait_recv()
    own = piece_of(0)
    total = near_sum[pl.ds(own, PIECE), :].astype(jnp.float32)
    for i in range(len(FAR)):
        total = total + far_in[i].astype(jnp.float32)
    spot = pl.ds(pl.multiple_of(mine + own, PIECE), PIECE)
    charge_ref[spot, :] = total.astype(charge_ref.dtype)

    spreads = [
        send(
            charge_ref.at[spot], charge_ref.at[spot],
            spread_send.at[i], spread_recv.at[i], rep=rep_of(4 * step),
        )
        for i, step in enumerate(FAR)
    ]
    for copy in spreads:
        copy.wait_recv()
    lasts = []
    for i, (step, other, first, rows, _) in enumerate(NEAR):
        block = charge_ref.at[pl.ds(mine + first, rows)]
        lasts.append(send(block, block, last_send.at[i], last_recv.at[i], rep=rep_of(step, other)))

    def pass_on(i, start, rows):
        block = pl.ds(start, rows)
        target = jnp.where(start < middle, below, above)
        return send(charge_ref.at[block], halo_ref.at[block], halo_send.at[i], halo_recv.at[i], slab=target)

    halos = [pass_on(len(NEAR), mine, CLASS_ROWS)]
    for i in ARRIVALS:
        step, other, first, rows, _ = NEAR[i]
        lasts[i].wait_recv()
        halos.append(pass_on(i, class_of(-step, other) + first, rows))
    for copy in guesses + halos:
        copy.wait_recv()
    for copy in near + far + spreads + lasts + guesses + halos:
        copy.wait_send()


def solve_kernel(
    counts_ref,
    cells_ref,
    guess_ref,
    guess_before_ref,
    guess_after_ref,
    charge_ref,
    halo_ref,
    out_ref,
    even,
    odd,
    charge,
    table,
):
    planes, side, _ = guess_ref.shape
    depth = guess_before_ref.shape[0]
    total = cells_ref.shape[1]
    inside = pl.ds(PAD, side)

    blank = jnp.zeros((PAD, LANES), jnp.float32)

    @pl.loop(0, planes + 2 * depth)
    def _(plane):
        for buffer in (even, odd):
            buffer[plane, pl.ds(0, PAD), :] = blank
            buffer[plane, pl.ds(PAD + side, PAD), :] = blank

    @pl.loop(0, depth)
    def _(plane):
        even[plane, inside, :] = guess_before_ref[plane]
        even[depth + planes + plane, inside, :] = guess_after_ref[plane]

    @pl.loop(0, planes)
    def _(plane):
        even[depth + plane, inside, :] = guess_ref[plane]
        charge[depth - 1 + plane] = charge_ref[plane].astype(jnp.float32)

    @pl.loop(0, depth - 1)
    def _(plane):
        charge[plane] = halo_ref[depth - 1 + plane].astype(jnp.float32)
        charge[depth - 1 + planes + plane] = halo_ref[plane].astype(jnp.float32)

    def beside(value):
        lane = lax.broadcasted_iota(jnp.int32, value.shape, 1)
        first, last = lane == 0, lane == LANES - 1
        left = jnp.where(first, 0.0, pltpu.roll(value, 1, 1))
        right = jnp.where(last, 0.0, pltpu.roll(value, LANES - 1, 1))
        return left, right

    buffers = (even, odd)
    for sweep, (previous, push) in enumerate(coefficients()):
        now, later = buffers[sweep % 2], buffers[(sweep + 1) % 2]

        for start in range(0, side, 64):
            rows = pl.ds(PAD + start, 64)
            lower = now[sweep, rows, :]
            value = now[sweep + 1, rows, :]
            for plane in range(sweep + 1, planes + 2 * depth - 1 - sweep):
                upper = now[plane + 1, rows, :]
                left, right = beside(value)
                around = now[plane, pl.ds(PAD + start - 1, 64), :] + now[plane, pl.ds(PAD + start + 1, 64), :]
                around = around + (lower + upper)
                around = around + charge[plane - 1, pl.ds(start, 64), :]
                fresh = push * (around + (left + right))
                if sweep:
                    fresh = fresh - previous * later[plane, rows, :]
                later[plane, rows, :] = fresh
                lower, value = value, upper

    final = buffers[SWEEPS % 2]
    for plane in range(planes):
        at = depth + plane
        spot = slice(plane * LANES, (plane + 1) * LANES)
        left, right = beside(final[at, inside, :])
        parts = (
            final[at, pl.ds(PAD - 1, side), :] - final[at, pl.ds(PAD + 1, side), :],
            left - right,
            final[at - 1, inside, :] - final[at + 1, inside, :],
        )
        for part, difference in enumerate(parts):
            table[part * side : (part + 1) * side, spot] = (difference * 0.5).astype(jnp.bfloat16)

    block = 256
    keys = lax.broadcasted_iota(jnp.int16, (planes * LANES, block), 0)
    ranks = lax.broadcasted_iota(jnp.int32, (side, block), 0)
    for start in range(0, total, block):
        cells = cells_ref[:, start : start + block]
        key = ((cells >> 14) << 7) | (cells & (LANES - 1))
        rank = (cells >> 7) & (LANES - 1)
        onehot = jnp.where(keys == key.astype(jnp.int16), jnp.bfloat16(1.0), jnp.bfloat16(0.0))
        picked = jnp.dot(table[...], onehot, preferred_element_type=jnp.float32)
        slot = lax.broadcasted_iota(jnp.int32, (1, block), 1) + start
        live = slot < counts_ref[0, 0]
        chosen = (ranks == rank) & live
        for part in range(3):
            values = jnp.where(chosen, picked[part * side : (part + 1) * side], 0.0)
            out_ref[part, :, start : start + block] = KICK_STRENGTH * jnp.sum(
                values, axis=0, keepdims=True
            )


def local(cells, charges, counts, potential_guess):
    planes, side, _ = potential_guess.shape
    total = cells.shape[1]
    depth = SWEEPS + 1
    vmem = pl.BlockSpec(memory_space=pltpu.VMEM)
    smem = pl.BlockSpec(memory_space=pltpu.SMEM)
    outside = pl.BlockSpec(memory_space=pl.ANY)
    params = pltpu.CompilerParams(vmem_limit_bytes=VMEM_LIMIT)

    rows = planes * side
    near = pltpu.SemaphoreType.DMA((len(NEAR),))
    far = pltpu.SemaphoreType.DMA((len(FAR),))
    halos = pltpu.SemaphoreType.DMA((len(NEAR) + 1,))
    pair = pltpu.SemaphoreType.DMA((2,))
    grid = jax.ShapeDtypeStruct((rows, LANES), jnp.bfloat16)
    ends = jax.ShapeDtypeStruct((depth, side, LANES), jnp.float32)
    charge, halo, guess_before, guess_after = pl.pallas_call(
        reduce_kernel,
        out_shape=[grid, grid, ends, ends],
        in_specs=[smem, vmem, vmem, outside],
        out_specs=[vmem, vmem, outside, outside],
        scratch_shapes=[
            pltpu.VMEM((rows, LANES), jnp.bfloat16),
            pltpu.VMEM((NEAR_SLOTS, CLASS_ROWS, LANES), jnp.bfloat16),
            pltpu.VMEM((CLASS_ROWS, LANES), jnp.bfloat16),
            pltpu.VMEM((len(FAR), PIECE, LANES), jnp.bfloat16),
            near, near, far, far, far, far, near, near, halos, halos, pair, pair,
        ],
        compiler_params=pltpu.CompilerParams(
            vmem_limit_bytes=VMEM_LIMIT, collective_id=0, has_side_effects=True
        ),
    )(counts, cells, charges, potential_guess)
    charge = charge.reshape(planes, side, LANES)
    halo = halo.reshape(planes, side, LANES)
    deep = planes + 2 * depth
    kicks = pl.pallas_call(
        solve_kernel,
        out_shape=jax.ShapeDtypeStruct((3, 1, total), jnp.float32),
        in_specs=[smem] + [vmem] * 6,
        out_specs=vmem,
        scratch_shapes=[
            pltpu.VMEM((deep, side + 2 * PAD, LANES), jnp.float32),
            pltpu.VMEM((deep, side + 2 * PAD, LANES), jnp.float32),
            pltpu.VMEM((deep - 2, side, LANES), jnp.float32),
            pltpu.VMEM((3 * side, planes * LANES), jnp.bfloat16),
        ],
        compiler_params=params,
    )(counts, cells, potential_guess, guess_before, guess_after, charge, halo)
    return kicks


def solution(mesh):
    return jax.shard_map(
        local,
        mesh=mesh,
        in_specs=(P("slab", "rep"), P("slab", "rep"), P("slab", "rep"), P("slab", None, None)),
        out_specs=P(None, "slab", "rep"),
        check_vma=False,
    )
```
